512 devices in a mesh: section: 32 (over z, core), mp: 16 (over y, x).
Axes of the slice: x: 4, y: 4, z: 16, core: 2. Of those that a mesh axis runs over, the one named last changes fastest.
Arguments:
- matches: int32 [4096, 2], P('section'), may hold values from 0 to 31, all different within a row; in each aligned block of 128 rows (0 to 127, 128 to 255, ...) at most 16 rows name the same one
- actions: int32 [2, 4096, 2], P(None, 'section'), may hold values from 0 to 1023
- state: float32 [4096, 2, 2048], P('section', None, 'mp'), may hold values from -6 to 6
- embed: bfloat16 [1024, 2048], P(None, 'mp'), may hold values from -3 to 3
- w_in: bfloat16 [32, 1, 2048, 8192], P('section', None, None, 'mp'), may hold values from -0.125 to 0.125
- w_out: bfloat16 [32, 1, 8192, 2048], P('section', None, 'mp'), may hold values from -0.0625 to 0.0625
- head: bfloat16 [32, 2048, 1024], P('section', None, 'mp'), may hold values from -16 to 16
Outputs:
- logp: float32 [2, 4096, 2], P(None, 'section')
The draws below stay inside these ranges and needn't reach their ends.
Inputs may be any that keep to these rules, and one draw needn't show every extreme that they name: `matches`: each game names two different agents; among the 128 games of one index of section no agent is named more than 16 times, a bound that some block reaches in some of these groups.
All inputs are finite; a program needn't handle non-finite values.
Results may differ from the reference program's by a relative error of at most 0.0095.
Values may be sent and summed in bfloat16 or wider, within the bound.
A program may use at most 64 MiB of HBM per device.

```python
import math
import jax
import jax.numpy as jnp
import numpy as np
from jax import lax

D = 2048
FF = 8192
ACTIONS = 1024
LAYERS = 1
STEPS = 2
GAMES_DEV = 128
AGENTS = 32
CAP = 16
SLOTS = 512
GAMES = 4096
N_MP = 16


def draw_head(key, part):
    key_base = jax.random.fold_in(key, 0)
    base = jax.random.normal(key_base, (AGENTS, D, ACTIONS), jnp.float32) * (3.0 / math.sqrt(D))
    return jnp.clip(base, -16.0, 16.0).astype(jnp.bfloat16)


def place_ends(entries, stream_key, least, high):
    dims = entries.shape
    index_at = [jax.random.randint(jax.random.fold_in(stream_key, axis), (), 0, dims[axis]) for axis in range(len(dims))]
    entries = entries.at[tuple(index_at)].set(least)
    longest = dims.index(max(dims))
    index_at[longest] = (index_at[longest] + 1) % dims[longest]
    return entries.at[tuple(index_at)].set(high)


def shard_levels(key, extent, cuts, low, high):
    loudness = 1.0
    for position, blocks in cuts:
        steps = jax.random.uniform(jax.random.fold_in(jax.random.fold_in(key, 6), position), (blocks,), jnp.float32, low / len(cuts), high / len(cuts))
        loudness = loudness * jnp.repeat(jnp.exp(steps), extent[position] // blocks).reshape((-1,) + (1,) * (len(extent) - 1 - position))
    return loudness


def deal_out(rng, own, number, rows, number_of, top, bound, skew):
    ranking = jax.random.permutation(rng, number_of)
    crowded, ordinary = load_shares(number_of, rows * top, bound, skew, True), load_shares(number_of, rows * top, bound, skew, False)
    places = jnp.arange(number_of)

    def named(lengths, turn):
        used = int((lengths > 0).sum())
        fixed = max(1, used // 4)
        shifted = fixed + (places - fixed + turn * (used - fixed)) % max(1, number_of - fixed)
        return jnp.zeros((number_of,), jnp.int32).at[ranking[jnp.where(places < fixed, places, shifted)]].set(jnp.asarray(lengths, jnp.int32))

    lengths = jnp.where(number % 4 == 0, named(crowded, number // 4), named(ordinary, number - number // 4 - 1))
    mixed = jax.random.permutation(jax.random.fold_in(own, 3), number_of)
    source_of, sink = mixed[0:number_of // 2 * 2:2], mixed[1:number_of // 2 * 2:2]
    slack = jnp.minimum(lengths[source_of] - 1, bound - lengths[sink]) // 2
    slack = jnp.where((source_of == ranking[0]) | (sink == ranking[0]) | (lengths[sink] == 0), 0, jnp.maximum(slack, 0))
    shifted = jax.random.randint(jax.random.fold_in(own, 4), (number_of // 2,), 0, 1 << 20) % (slack + 1)
    lengths = lengths.at[source_of].add(-shifted).at[sink].add(shifted)
    labels = jnp.searchsorted(jnp.cumsum(lengths), jnp.arange(rows * top), side="right").astype(jnp.int32)
    table = labels.reshape(top, rows).T
    table = table[jax.random.permutation(jax.random.fold_in(own, 1), rows)]
    turn = jax.random.randint(jax.random.fold_in(own, 2), (rows, 1), 0, top)
    return jnp.take_along_axis(table, (jnp.arange(top)[None, :] + turn) % top, axis=1)


def load_shares(amount, total, bound, lean, full):
    loads = [(1 << 20) // math.isqrt(grade ** lean) + 1 for grade in range(1, amount + 1)]
    largest = bound if full else min(bound, max(-(-total // amount), total * loads[0] // sum(loads)))
    least = 1 if total - largest >= amount - 1 else 0
    given, rest = [largest] + [least] * (amount - 1), total - largest - least * (amount - 1)
    while rest > 0:
        free = [i for i in range(1, amount) if given[i] < largest] or [i for i in range(1, amount) if given[i] < bound]
        mass, budget = sum([loads[i] for i in free]), rest
        for i in free:
            extra = min(bound - given[i], max(1, budget * loads[i] // mass), rest)
            given[i] = given[i] + extra
            rest = rest - extra
    return np.array(given)


def centred(own_key, shape, width, bound, cuts=(), kind=jnp.bfloat16):
    array = jax.random.normal(own_key, shape, jnp.float32) * width
    if len(cuts) > 0:
        array = shard_levels(own_key, shape, cuts, -0.22, 0.18) * array
    return jnp.clip(array, min=-bound, max=bound).astype(kind)


def setup_inputs(seed: int = 0) -> dict:
    seeds = jax.random.split(jax.random.key(seed), 8)
    matches_keys = jax.random.split(jax.random.fold_in(seeds[0], 1), GAMES // GAMES_DEV)
    matches_turns = jax.random.permutation(jax.random.fold_in(seeds[0], 3), GAMES // GAMES_DEV)
    matches = jax.vmap(lambda own, number: deal_out(jax.random.fold_in(seeds[0], 2), own, number, GAMES_DEV, AGENTS, 2, CAP, 2))(matches_keys, matches_turns).reshape((GAMES, 2))
    actions = place_ends(jax.random.randint(seeds[1], (STEPS, GAMES, 2), 0, ACTIONS), jax.random.fold_in(seeds[1], 1), 0, ACTIONS - 1).astype(jnp.int32)
    state = centred(seeds[2], (GAMES, 2, D), 1.0, 6.0, ((0, 32), (2, 16)), jnp.float32)
    embed = centred(seeds[3], (ACTIONS, D), 0.5, 3.0, ((1, 16),))
    w_in = centred(seeds[4], (AGENTS, LAYERS, D, FF), D ** -0.5, 0.125, ((0, 32), (3, 16)))
    w_out = centred(seeds[5], (AGENTS, LAYERS, FF, D), FF ** -0.5, 0.0625, ((0, 32), (2, 16)))
    head = draw_head(jax.random.fold_in(seeds[7], 71), 0)
    return {"matches": matches, "actions": actions, "state": state, "embed": embed, "w_in": w_in, "w_out": w_out, "head": head}


norm_eps = 1e-06

def rms_round(source):
    widened = source.astype(jnp.float32)
    scale = lax.rsqrt(lax.optimization_barrier(jnp.mean(widened * widened, axis=-1, keepdims=True)) + norm_eps)
    return (widened * scale).astype(jnp.bfloat16)

def agent_logits(row_block, in_weights, out_weights, head_weights):
    layer_in = row_block
    summed = row_block.astype(jnp.float32)
    for layer_idx in range(LAYERS):
        normed = rms_round(layer_in)
        hidden = jax.nn.gelu(jnp.dot(normed, in_weights[layer_idx], preferred_element_type=jnp.float32)).astype(jnp.bfloat16)
        groups = hidden.astype(jnp.float32).reshape(hidden.shape[0], N_MP, FF // N_MP)
        blocks = out_weights[layer_idx].astype(jnp.float32).reshape(N_MP, FF // N_MP, D)
        partial_value = jnp.einsum('bmf,mfd->bmd', groups, blocks).astype(jnp.bfloat16)
        partial_value = lax.optimization_barrier(partial_value).astype(jnp.float32)
        summed = layer_in.astype(jnp.float32) + lax.optimization_barrier(jnp.sum(partial_value, axis=1))
        if layer_idx + 1 < LAYERS:
            layer_in = summed.astype(jnp.bfloat16)
    return jnp.dot(rms_round(summed), head_weights, preferred_element_type=jnp.float32)

def reference(matches, actions, state, embed, w_in, w_out, head):
    owners = matches.reshape(-1).astype(jnp.int32)
    total_rows = owners.shape[0]
    row_order = jnp.argsort(owners, stable=True).astype(jnp.int32)
    counts = lax.optimization_barrier(jnp.sum((owners[:, None] == jnp.arange(AGENTS, dtype=jnp.int32)[None, :]).astype(jnp.int32), axis=0))
    starts = (jnp.cumsum(counts) - counts).astype(jnp.int32)
    padded_order = jnp.concatenate([row_order, jnp.zeros((SLOTS,), jnp.int32)])
    current = state
    results = []
    for step_idx in range(STEPS):
        rows_all = current.reshape(total_rows, D).astype(jnp.bfloat16)
        chosen = actions[step_idx].reshape(-1).astype(jnp.int32)

        def serve_agent(packed):
            agent_id, in_weights, out_weights, head_weights = packed
            row_index = lax.dynamic_slice(padded_order, (starts[agent_id],), (SLOTS,)).astype(jnp.int32)
            is_live = jnp.arange(SLOTS, dtype=jnp.int32) < counts[agent_id]
            logits = agent_logits(rows_all[row_index], in_weights, out_weights, head_weights)
            row_peak = lax.optimization_barrier(jnp.max(logits, axis=1, keepdims=True))
            row_total = lax.optimization_barrier(jnp.sum(jnp.exp(logits - row_peak), axis=1))
            picked = jnp.take_along_axis(logits, chosen[row_index][:, None], axis=1)[:, 0]
            row_value = picked - row_peak[:, 0] - jnp.log(row_total)
            return (jnp.where(is_live, row_value, 0.0), jnp.where(is_live, row_index, total_rows))
        row_values, targets = lax.map(serve_agent, (jnp.arange(AGENTS, dtype=jnp.int32), w_in, w_out, head))
        logp = jnp.zeros((total_rows + 1,), jnp.float32).at[targets.reshape(-1)].add(row_values.reshape(-1))[:total_rows]
        results.append(logp.reshape(GAMES, 2))
        picked_rows = jnp.take(embed, actions[step_idx], axis=0).astype(jnp.float32)
        current = 0.8 * current + picked_rows + 0.5 * picked_rows[:, ::-1, :]
    return jnp.stack(results)
```

```python
import jax
import jax.numpy as jnp
from jax import lax
from jax.experimental import pallas as pl
from jax.experimental.pallas import tpu as pltpu
from jax.sharding import PartitionSpec as P

STEPS = 2
SIDE = 4
EPS = 1e-06
MESH = pl.DeviceIdType.MESH
F32 = jnp.float32
BF16 = jnp.bfloat16

OFFS = (0, -1, 1, 2)


def wrap(pos, off):
    return lax.rem(pos + (off + SIDE), SIDE) if off else pos


class Plane:
    def __init__(self):
        self.mp = lax.axis_index("mp")
        self.y = self.mp // SIDE
        self.x = lax.rem(self.mp, SIDE)

    def at(self, half, da, db):
        if half == 0:
            return wrap(self.y, db) * SIDE + wrap(self.x, da)
        return wrap(self.y, da) * SIDE + wrap(self.x, db)

    def peer(self, half, ring, step):
        return self.at(half, step, 0) if ring == 0 else self.at(half, 0, step)


class Gather:
    def __init__(self, plane, buf, rsem, ssem):
        self.plane, self.buf, self.rsem, self.ssem = plane, buf, rsem, ssem
        self.rows = buf.shape[1]

    def copy(self, half, event, ring, step, da, db, part):
        quarter = self.rows // 4
        start = half * 2 * quarter + (quarter if part == 2 else 0)
        size = 2 * quarter if part == 0 else quarter
        ref = self.buf.at[self.plane.at(half, da, db), pl.ds(start, size), :]
        return pltpu.make_async_remote_copy(
            src_ref=ref,
            dst_ref=ref,
            send_sem=self.ssem,
            recv_sem=self.rsem.at[half * 20 + event],
            device_id={"mp": self.plane.peer(half, ring, step)},
            device_id_type=MESH,
        )

    def own(self, half):
        self.copy(half, 0, 0, 1, 0, 0, 0).start()
        self.copy(half, 1, 0, -1, 0, 0, 0).start()
        self.across(half, 0)

    def across(self, half, k):
        self.copy(half, 4 + 4 * k, 1, 1, OFFS[k], 0, 0).start()
        self.copy(half, 5 + 4 * k, 1, -1, OFFS[k], 0, 0).start()

    def first(self, half):
        self.copy(half, 0, 0, 1, -1, 0, 0).wait_recv()
        self.copy(half, 2, 0, 1, -1, 0, 1).start()
        self.across(half, 1)
        self.copy(half, 1, 0, -1, 1, 0, 0).wait_recv()
        self.copy(half, 3, 0, -1, 1, 0, 2).start()
        self.across(half, 2)

    def second(self, half):
        self.copy(half, 2, 0, 1, 2, 0, 1).wait_recv()
        self.copy(half, 3, 0, -1, 2, 0, 2).wait_recv()
        self.across(half, 3)

    def pass_on(self, half, k):
        self.copy(half, 4 + 4 * k, 1, 1, OFFS[k], -1, 0).wait_recv()
        self.copy(half, 6 + 4 * k, 1, 1, OFFS[k], -1, 1).start()
        self.copy(half, 5 + 4 * k, 1, -1, OFFS[k], 1, 0).wait_recv()
        self.copy(half, 7 + 4 * k, 1, -1, OFFS[k], 1, 2).start()

    def last(self, half, k):
        self.copy(half, 6 + 4 * k, 1, 1, OFFS[k], 2, 1).wait_recv()
        self.copy(half, 7 + 4 * k, 1, -1, OFFS[k], 2, 2).wait_recv()

    def sent(self):
        ref = self.buf.at[pl.ds(0, SIDE * SIDE - 1)]
        pltpu.make_async_copy(ref, ref, self.ssem).wait()


class RingSum:
    def __init__(self, plane, half, ring, src, relay, acc, dst, ssem, rsem, base):
        self.plane, self.half, self.ring = plane, half, ring
        self.src, self.relay, self.acc, self.dst = src, relay, acc, dst
        self.ssem, self.rsem, self.base = ssem, rsem, base
        self.cut = src.shape[1] // 2

    def send(self, event, step, src, dst):
        return pltpu.make_async_remote_copy(
            src_ref=src,
            dst_ref=dst,
            send_sem=self.ssem.at[self.base + event],
            recv_sem=self.rsem.at[self.base + event],
            device_id={"mp": self.plane.peer(self.half, self.ring, step)},
            device_id_type=MESH,
        )

    def lo(self, ref, k):
        return ref.at[k, pl.ds(0, self.cut)]

    def hi(self, ref, k):
        return ref.at[k, pl.ds(self.cut, self.cut)]

    def copies(self):
        src, dst = self.src, self.dst
        return (
            self.send(0, 1, self.lo(src, 3), self.relay.at[0]),
            self.send(1, -1, self.hi(src, 3), self.relay.at[1]),
            self.send(2, 1, self.hi(src, 2), self.hi(dst, 0)),
            self.send(3, -1, self.lo(src, 1), self.lo(dst, 1)),
            self.send(4, 1, self.acc.at[0], self.lo(dst, 0)),
            self.send(5, -1, self.acc.at[1], self.hi(dst, 1)),
        )

    def far(self):
        both = self.copies()
        both[0].start()
        both[1].start()

    def near(self):
        both = self.copies()
        both[2].start()
        both[3].start()

    def join(self):
        both = self.copies()
        both[0].wait_recv()
        self.acc[0] = (self.lo(self.src, 2)[...].astype(F32) + self.relay[0].astype(F32)).astype(BF16)
        both[4].start()
        both[1].wait_recv()
        self.acc[1] = (self.hi(self.src, 1)[...].astype(F32) + self.relay[1].astype(F32)).astype(BF16)
        both[5].start()

    def arrive(self):
        for copy in self.copies()[2:]:
            copy.wait_recv()

    def sent(self):
        for copy in self.copies():
            copy.wait_send()


def body(
    orow_ref, ocol_ref, acts_ref, state_ref, embed_ref, w_in_hbm, w_out_hbm, head_hbm,
    out_ref,
    zsend, asend, aland, xbuf, hbuf, w_in, w_out, accum, squares, hid,
    part0, part1, relay0, relay1, acc0, acc1, dst0, dst1,
    sub0, sub1, srelay0, srelay1, sacc0, sacc1, sdst0, sdst1, keep,
    rsend, rland,
    wsem, zsem, asem, xrsem, xssem, hrsem, hssem, rs_s, rs_r, bsem,
):
    plane = Plane()
    mp = plane.mp
    sections = lax.axis_size("section")
    me = lax.axis_index("section")
    rows = orow_ref.shape[1]
    cap = zsend.shape[1] // STEPS
    block = STEPS * cap
    agents = sections

    barrier = pltpu.get_barrier_semaphore()

    def greet(i, _):
        pl.semaphore_signal(
            barrier, inc=1, device_id={"section": lax.rem(me + i, sections)}, device_id_type=MESH
        )
        return 0

    lax.fori_loop(1, sections, greet, 0)
    for ring in (0, 1):
        for step in (1, -1):
            pl.semaphore_signal(
                barrier, inc=1, device_id={"mp": plane.peer(0, ring, step)}, device_id_type=MESH
            )

    load_head = pltpu.make_async_copy(head_hbm, hbuf.at[mp], wsem.at[0])
    load_in = pltpu.make_async_copy(w_in_hbm, w_in, wsem.at[1])
    load_out = pltpu.make_async_copy(w_out_hbm, w_out, wsem.at[2])
    load_head.start()
    load_in.start()
    load_out.start()

    orow, ocol = orow_ref[...], ocol_ref[...]
    same = orow == ocol
    sub = lax.broadcasted_iota(jnp.int32, (rows, rows), 0)
    lane = lax.broadcasted_iota(jnp.int32, (rows, rows), 1)
    rank_col = jnp.sum(jnp.where(same & (lane < sub), 1.0, 0.0), axis=1, keepdims=True).astype(jnp.int32)
    rank_row = jnp.sum(jnp.where(same & (sub < lane), 1.0, 0.0), axis=0, keepdims=True).astype(jnp.int32)
    place = orow * cap + rank_row
    pick = jnp.where(
        lax.broadcasted_iota(jnp.int32, (agents * cap, rows), 0) == place, 1.0, 0.0
    ).astype(BF16)
    owner = jnp.where(lax.broadcasted_iota(jnp.int32, (agents, rows), 0) == orow, 1.0, 0.0)

    view = state_ref[...]
    table = lax.broadcasted_iota(jnp.int32, (rows, embed_ref.shape[0]), 1)
    mix = jnp.where(table == acts_ref[:, 0:1], 1.0, 0.0) + jnp.where(table == acts_ref[:, 2:3], 0.5, 0.0)
    later = 0.8 * view + jnp.dot(mix.astype(BF16), embed_ref[...], preferred_element_type=F32)
    width = view.shape[1]
    for step, seen in enumerate((view, later)):
        routed = jnp.dot(pick, seen.astype(BF16), preferred_element_type=F32).astype(BF16)
        zsend[:, step * cap:(step + 1) * cap, :] = routed.reshape(agents, cap, width)

    spot = lax.broadcasted_iota(jnp.int32, (rows, 128), 1)
    value = jnp.where(spot < cap, acts_ref[:, 0:1], acts_ref[:, 1:2])
    hit = (jnp.where(spot < cap, spot, spot - cap) == rank_col) & (spot < block)
    high = jnp.where(hit, value // 32, 0).astype(F32).astype(BF16)
    low = jnp.where(hit, value % 32, 0).astype(F32).astype(BF16)
    owner16 = owner.astype(BF16)
    named = 32.0 * jnp.dot(owner16, high, preferred_element_type=F32) + jnp.dot(
        owner16, low, preferred_element_type=F32
    )
    asend[...] = named.reshape(agents, 1, 128)

    pl.semaphore_wait(barrier, sections - 1 + 4)

    def zcopy(agent):
        return pltpu.make_async_remote_copy(
            src_ref=zsend.at[agent],
            dst_ref=xbuf.at[mp, pl.ds(pl.multiple_of(me * block, block), block), :],
            send_sem=zsem.at[0],
            recv_sem=zsem.at[1],
            device_id={"section": agent},
            device_id_type=MESH,
        )

    def route(i, _):
        zcopy(lax.rem(me + i, sections)).start()
        return 0

    load_head.wait()
    head = Gather(plane, hbuf, hrsem, hssem)
    for half in (0, 1):
        head.own(half)
    lax.fori_loop(1, sections, route, 0)
    here = pltpu.make_async_copy(
        zsend.at[me],
        xbuf.at[mp, pl.ds(pl.multiple_of(me * block, block), block), :],
        zsem.at[1],
    )
    here.start()

    per = sections // (SIDE * SIDE)

    def acopy(agent):
        return pltpu.make_async_remote_copy(
            src_ref=asend.at[agent],
            dst_ref=aland.at[lax.rem(me, per)],
            send_sem=asem.at[0],
            recv_sem=asem.at[1],
            device_id={"section": agent},
            device_id_type=MESH,
        )

    def tell(i, _):
        acopy(lax.rem(me + i, sections)).start()
        return 0

    @pl.when(me // per == mp)
    def _():
        lax.fori_loop(1, sections, tell, 0)
        pltpu.make_async_copy(asend.at[me], aland.at[lax.rem(me, per)], asem.at[1]).start()

    for half in (0, 1):
        head.first(half)
    for half in (0, 1):
        head.pass_on(half, 0)
    for half in (0, 1):
        head.second(half)

    pltpu.make_async_copy(xbuf.at[mp], xbuf.at[mp], zsem.at[1]).wait()
    inputs = Gather(plane, xbuf, xrsem, xssem)
    for half in (0, 1):
        inputs.own(half)
    for k in (1, 2, 3):
        for half in (0, 1):
            head.pass_on(half, k)
    load_in.wait()
    load_out.wait()
    for half in (0, 1):
        inputs.first(half)
    for half in (0, 1):
        inputs.pass_on(half, 0)
    for half in (0, 1):
        inputs.second(half)

    span = xbuf.shape[1] // 2

    def project(half, db, fresh):
        index = [plane.at(half, da, db) for da in OFFS]
        lhs = jnp.concatenate([xbuf[i, half * span:(half + 1) * span, :] for i in index], axis=1)
        rhs = jnp.concatenate(
            [w_in[pl.ds(pl.multiple_of(i * width, width), width), :] for i in index], axis=0
        )
        total = jnp.dot(lhs, rhs, preferred_element_type=F32)
        wide = lhs.astype(F32)
        wide = wide * wide
        square = sum(wide[:, j * width:(j + 1) * width] for j in range(SIDE))
        if fresh:
            accum[half] = total
            squares[half] = square
        else:
            accum[half] += total
            squares[half] += square

    for half in (0, 1):
        project(half, 0, True)
    for k in (1, 2, 3):
        for half in (0, 1):
            inputs.pass_on(half, k)
    for half in (0, 1):
        project(half, -1, False)
        project(half, 1, False)
    features = width * SIDE * SIDE
    chunks = SIDE * SIDE
    each = xbuf.shape[1] // chunks
    for half in (0, 1):
        for k in range(4):
            inputs.last(half, k)
        project(half, 2, False)
        scale = lax.rsqrt(jnp.sum(squares[half], axis=1, keepdims=True) * (1.0 / features) + EPS)
        hidden = jax.nn.gelu(accum[half] * scale).astype(BF16)
        hid[half * chunks // 2:(half + 1) * chunks // 2] = hidden.reshape(chunks // 2, each, hidden.shape[1])

    outer = [
        RingSum(plane, 0, 0, part0, relay0, acc0, dst0, rs_s, rs_r, 0),
        RingSum(plane, 1, 0, part1, relay1, acc1, dst1, rs_s, rs_r, 6),
    ]
    inner = [
        RingSum(plane, 0, 1, sub0, srelay0, sacc0, sdst0, rs_s, rs_r, 12),
        RingSum(plane, 1, 1, sub1, srelay1, sacc1, sdst1, rs_s, rs_r, 18),
    ]
    parts = (part0, part1)
    subs = (sub0, sub1)
    dsts = (dst0, dst1)
    sdsts = (sdst0, sdst1)
    wide_cols = w_out.shape[1] // 2

    def expand(half, k):
        if half == 0:
            index = [b * SIDE + wrap(plane.x, OFFS[k]) for b in range(SIDE)]
        else:
            index = [wrap(plane.y, OFFS[k]) * SIDE + b for b in range(SIDE)]
        lhs = jnp.concatenate([hid[i] for i in index], axis=0)
        total = jnp.dot(
            lhs, w_out[:, half * wide_cols:(half + 1) * wide_cols], preferred_element_type=F32
        )
        parts[half][k] = total.astype(BF16).reshape(SIDE, each, wide_cols)

    for half in (0, 1):
        expand(half, 3)
        outer[half].far()
    for half in (0, 1):
        expand(half, 1)
        expand(half, 2)
        outer[half].near()
    for half in (0, 1):
        expand(half, 0)
    for half in (0, 1):
        outer[half].join()

    def fold(half, k):
        b = wrap(plane.y if half == 0 else plane.x, OFFS[k])
        return (
            parts[half][0, b].astype(F32) + dsts[half][0, b].astype(F32) + dsts[half][1, b].astype(F32)
        )

    for half in (0, 1):
        outer[half].arrive()
        subs[half][3] = fold(half, 3).astype(BF16)
        inner[half].far()
        subs[half][1] = fold(half, 1).astype(BF16)
        subs[half][2] = fold(half, 2).astype(BF16)
        inner[half].near()
        keep[half] = fold(half, 0)
    for half in (0, 1):
        inner[half].join()
    for half in (0, 1):
        for k in range(4):
            head.last(half, k)
    rest = []
    for half in (0, 1):
        inner[half].arrive()
        rest.append(keep[half] + sdsts[half][0].astype(F32) + sdsts[half][1].astype(F32))

    mine = pl.ds(pl.multiple_of(mp * each, each), each)
    source = jnp.concatenate([xbuf[j, mine, :] for j in range(chunks)], axis=1).astype(F32)
    summed = source + jnp.concatenate(rest, axis=1)
    scale = lax.rsqrt(jnp.mean(summed * summed, axis=1, keepdims=True) + EPS)
    normed = (summed * scale).astype(BF16)
    scores = lax.dot_general(
        normed,
        hbuf[...].reshape(chunks * hbuf.shape[1], features),
        (((1,), (1,)), ((), ())),
        preferred_element_type=F32,
    )
    pltpu.make_async_copy(aland, aland, asem.at[1]).wait()
    peak = jnp.max(scores, axis=1, keepdims=True)
    total = jnp.sum(jnp.exp(scores - peak), axis=1, keepdims=True)
    ident = lax.broadcasted_iota(jnp.int32, (block, 128), 0) == lax.broadcasted_iota(
        jnp.int32, (block, 128), 1
    )
    chosen = jnp.concatenate(
        [jnp.sum(jnp.where(ident, aland[c], 0.0), axis=1, keepdims=True) for c in range(per)], axis=0
    )
    names = lax.broadcasted_iota(jnp.int32, scores.shape, 1)
    taken = jnp.sum(jnp.where(names == chosen.astype(jnp.int32), scores, 0.0), axis=1, keepdims=True)
    logp = taken - peak - jnp.log(total)
    for c in range(per):
        piece = logp[c * block:(c + 1) * block]
        rsend[c] = jnp.sum(jnp.where(ident, piece, 0.0), axis=0, keepdims=True)

    def rcopy(c, dest):
        return pltpu.make_async_remote_copy(
            src_ref=rsend.at[c],
            dst_ref=rland.at[me],
            send_sem=bsem.at[0],
            recv_sem=bsem.at[1],
            device_id={"section": mp * per + c, "mp": dest},
            device_id_type=MESH,
        )

    def give(i, _):
        c = i // chunks
        dest = lax.rem(i, chunks)
        self_copy = (mp * per + c == me) & (dest == mp)

        @pl.when(jnp.logical_not(self_copy))
        def _():
            rcopy(c, dest).start()

        @pl.when(self_copy)
        def _():
            pltpu.make_async_copy(rsend.at[c], rland.at[me], bsem.at[1]).start()

        return 0

    lax.fori_loop(0, per * chunks, give, 0)
    pltpu.make_async_copy(rland, rland, bsem.at[1]).wait()

    back = rland[...].reshape(agents, 128)
    spread = lax.dot_general(
        back, owner, (((0,), (0,)), ((), ())), precision=lax.Precision.HIGHEST, preferred_element_type=F32
    )
    slot = lax.broadcasted_iota(jnp.int32, (128, rows), 0)
    for step in range(STEPS):
        out_ref[step:step + 1, :] = jnp.sum(
            jnp.where(slot == rank_row + step * cap, spread, 0.0), axis=0, keepdims=True
        )

    full = zsend.at[pl.ds(0, sections - 1)]
    pltpu.make_async_copy(full, full, zsem.at[0]).wait()

    @pl.when(me // per == mp)
    def _():
        told = asend.at[pl.ds(0, sections - 1)]
        pltpu.make_async_copy(told, told, asem.at[0]).wait()

    head.sent()
    inputs.sent()
    for half in (0, 1):
        outer[half].sent()
        inner[half].sent()
    given = rland.at[pl.ds(0, per * chunks - 1)]
    pltpu.make_async_copy(given, given, bsem.at[0]).wait()

    @pl.when(me // per != mp)
    def _():
        one = rland.at[0]
        pltpu.make_async_copy(one, one, bsem.at[0]).wait()


def per_device(matches, actions, state, embed, w_in, w_out, head):
    sections = lax.axis_size("section")
    games = matches.shape[0]
    rows = 2 * games
    width = state.shape[2]
    cap = 4 * games // sections
    served = sections * STEPS * cap
    chunks = SIDE * SIDE
    each = served // chunks
    hidden = w_in.shape[3]
    features = w_in.shape[2]
    columns = head.shape[2]
    half_cols = features // 2
    owners = matches.reshape(-1)
    opposite = actions[0, :, ::-1].reshape(-1)
    acts = jnp.stack([actions[0].reshape(-1), actions[1].reshape(-1), opposite], axis=1)
    vmem = pl.BlockSpec(memory_space=pltpu.VMEM)
    hbm = pl.BlockSpec(memory_space=pl.ANY)
    per = sections // chunks
    part = pltpu.VMEM((4, SIDE, each, half_cols), BF16)
    pair = pltpu.VMEM((2, SIDE // 2, each, half_cols), BF16)
    dst = pltpu.VMEM((2, SIDE, each, half_cols), BF16)
    sub = pltpu.VMEM((4, each, half_cols), BF16)
    spair = pltpu.VMEM((2, each // 2, half_cols), BF16)
    sdst = pltpu.VMEM((2, each, half_cols), BF16)
    dma = pltpu.SemaphoreType.DMA
    out = pl.pallas_call(
        body,
        out_shape=jax.ShapeDtypeStruct((STEPS, rows), F32),
        in_specs=[vmem] * 5 + [hbm] * 3,
        out_specs=vmem,
        scratch_shapes=[
            pltpu.VMEM((sections, STEPS * cap, width), BF16),
            pltpu.VMEM((sections, 1, 128), F32),
            pltpu.VMEM((per, 1, 128), F32),
            pltpu.VMEM((chunks, served, width), BF16),
            pltpu.VMEM((chunks, columns, features), BF16),
            pltpu.VMEM((features, hidden), BF16),
            pltpu.VMEM((hidden, features), BF16),
            pltpu.VMEM((2, served // 2, hidden), F32),
            pltpu.VMEM((2, served // 2, width), F32),
            pltpu.VMEM((chunks, each, hidden), BF16),
            part, part, pair, pair, pair, pair, dst, dst,
            sub, sub, spair, spair, spair, spair, sdst, sdst,
            pltpu.VMEM((2, each, half_cols), F32),
            pltpu.VMEM((per, 1, 128), F32),
            pltpu.VMEM((sections, 1, 128), F32),
            dma((3,)), dma((2,)), dma((2,)),
            dma((40,)), dma, dma((40,)), dma,
            dma((24,)), dma((24,)), dma((2,)),
        ],
        compiler_params=pltpu.CompilerParams(
            collective_id=0, has_side_effects=True, vmem_limit_bytes=60 * 1024 * 1024
        ),
        name="league",
    )(
        owners.reshape(1, rows),
        owners.reshape(rows, 1),
        acts,
        state.reshape(rows, width),
        embed,
        w_in[0, 0],
        w_out[0, 0],
        head[0].T,
    )
    return out.reshape(STEPS, games, 2)


def solution(mesh):
    return jax.shard_map(
        per_device,
        mesh=mesh,
        in_specs=(
            P("section", None),
            P(None, "section", None),
            P("section", None, "mp"),
            P(None, "mp"),
            P("section", None, None, "mp"),
            P("section", None, "mp", None),
            P("section", None, "mp"),
        ),
        out_specs=P(None, "section", None),
        check_vma=False,
    )
```

```python
import jax
import jax.numpy as jnp
from jax import lax
from jax.experimental import pallas as pl
from jax.experimental.pallas import tpu as pltpu
from jax.sharding import PartitionSpec as P

STEPS = 2
SIDE = 4
EPS = 1e-06
MESH = pl.DeviceIdType.MESH
F32 = jnp.float32
BF16 = jnp.bfloat16

OFFS = (0, -1, 1, 2)


def wrap(pos, off):
    return lax.rem(pos + (off + SIDE), SIDE) if off else pos


class Plane:
    def __init__(self):
        self.mp = lax.axis_index("mp")
        self.y = self.mp // SIDE
        self.x = lax.rem(self.mp, SIDE)

    def at(self, half, da, db):
        if half == 0:
            return wrap(self.y, db) * SIDE + wrap(self.x, da)
        return wrap(self.y, da) * SIDE + wrap(self.x, db)

    def peer(self, half, ring, step):
        return self.at(half, step, 0) if ring == 0 else self.at(half, 0, step)


class Gather:
    def __init__(self, plane, buf, rsem, ssem):
        self.plane, self.buf, self.rsem, self.ssem = plane, buf, rsem, ssem
        self.rows = buf.shape[1]

    def copy(self, half, event, ring, step, da, db, part):
        quarter = self.rows // 4
        start = half * 2 * quarter + (quarter if part == 2 else 0)
        size = 2 * quarter if part == 0 else quarter
        ref = self.buf.at[self.plane.at(half, da, db), pl.ds(start, size), :]
        return pltpu.make_async_remote_copy(
            src_ref=ref,
            dst_ref=ref,
            send_sem=self.ssem,
            recv_sem=self.rsem.at[half * 20 + event],
            device_id={"mp": self.plane.peer(half, ring, step)},
            device_id_type=MESH,
        )

    def own(self, half):
        self.copy(half, 0, 0, 1, 0, 0, 0).start()
        self.copy(half, 1, 0, -1, 0, 0, 0).start()
        self.across(half, 0)

    def across(self, half, k):
        self.copy(half, 4 + 4 * k, 1, 1, OFFS[k], 0, 0).start()
        self.copy(half, 5 + 4 * k, 1, -1, OFFS[k], 0, 0).start()

    def first(self, half):
        self.copy(half, 0, 0, 1, -1, 0, 0).wait_recv()
        self.copy(half, 2, 0, 1, -1, 0, 1).start()
        self.across(half, 1)
        self.copy(half, 1, 0, -1, 1, 0, 0).wait_recv()
        self.copy(half, 3, 0, -1, 1, 0, 2).start()
        self.across(half, 2)

    def second(self, half):
        self.copy(half, 2, 0, 1, 2, 0, 1).wait_recv()
        self.copy(half, 3, 0, -1, 2, 0, 2).wait_recv()
        self.across(half, 3)

    def pass_on(self, half, k):
        self.copy(half, 4 + 4 * k, 1, 1, OFFS[k], -1, 0).wait_recv()
        self.copy(half, 6 + 4 * k, 1, 1, OFFS[k], -1, 1).start()
        self.copy(half, 5 + 4 * k, 1, -1, OFFS[k], 1, 0).wait_recv()
        self.copy(half, 7 + 4 * k, 1, -1, OFFS[k], 1, 2).start()

    def last(self, half, k):
        self.copy(half, 6 + 4 * k, 1, 1, OFFS[k], 2, 1).wait_recv()
        self.copy(half, 7 + 4 * k, 1, -1, OFFS[k], 2, 2).wait_recv()

    def sent(self):
        ref = self.buf.at[pl.ds(0, SIDE * SIDE - 1)]
        pltpu.make_async_copy(ref, ref, self.ssem).wait()


class RingSum:
    def __init__(self, plane, half, ring, src, relay, acc, dst, ssem, rsem):
        self.plane, self.half, self.ring = plane, half, ring
        self.src, self.relay, self.acc, self.dst = src, relay, acc, dst
        self.ssem, self.rsem = ssem, rsem
        self.cut = src.shape[1] // 2

    def copy(self, event):
        step = (1, -1)[event % 2]
        src, dst = self.src, self.dst
        lo, hi = pl.ds(0, self.cut), pl.ds(self.cut, self.cut)
        source, target = (
            lambda: (src.at[3, lo], self.relay.at[0]),
            lambda: (src.at[3, hi], self.relay.at[1]),
            lambda: (src.at[2, hi], dst.at[0, hi]),
            lambda: (src.at[1, lo], dst.at[1, lo]),
            lambda: (self.acc.at[0], dst.at[0, lo]),
            lambda: (self.acc.at[1], dst.at[1, hi]),
        )[event]()
        return pltpu.make_async_remote_copy(
            src_ref=source,
            dst_ref=target,
            send_sem=self.ssem,
            recv_sem=self.rsem.at[event],
            device_id={"mp": self.plane.peer(self.half, self.ring, step)},
            device_id_type=MESH,
        )

    def far(self):
        self.copy(0).start()
        self.copy(1).start()

    def near(self):
        self.copy(2).start()
        self.copy(3).start()

    def join(self):
        lo, hi = pl.ds(0, self.cut), pl.ds(self.cut, self.cut)
        self.copy(0).wait_recv()
        self.acc[0] = (self.src[2, lo].astype(F32) + self.relay[0].astype(F32)).astype(BF16)
        self.copy(4).start()
        self.copy(1).wait_recv()
        self.acc[1] = (self.src[1, hi].astype(F32) + self.relay[1].astype(F32)).astype(BF16)
        self.copy(5).start()

    def arrive(self):
        for event in range(2, 6):
            self.copy(event).wait_recv()

    def sent(self):
        ref = self.src.at[pl.ds(0, 3)]
        pltpu.make_async_copy(ref, ref, self.ssem).wait()


def body(
    matches_ref, actions_ref, state_ref, embed_ref, w_in_hbm, w_out_hbm, head_hbm,
    out_ref,
    zsend0, zsend1, asend, aland, xbuf0, xbuf1, hbuf0, hbuf1, w_in, w_out, hid,
    part, relay, acc, dst, sub, srelay, sacc, sdst, keep,
    rsend, rland,
    wsem, zsend_sem, zland_sem, asem, grsem, gssem, rs_s, rs_r, bsend_sem, bland_sem,
):
    plane = Plane()
    mp = plane.mp
    sections = lax.axis_size("section")
    me = lax.axis_index("section")
    games = matches_ref.shape[1]
    rows = 2 * games
    cap = zsend0.shape[1]
    agents = sections
    chunks = SIDE * SIDE
    per = sections // chunks
    zsends, xbufs, hbufs = (zsend0, zsend1), (xbuf0, xbuf1), (hbuf0, hbuf1)
    width = embed_ref.shape[1]
    features = width * chunks

    def other(i):
        k = sections - i
        odd, far = lax.rem(k, 2), (k + 1) // 2
        return lax.rem(me + odd * far + (1 - odd) * (sections - far), sections)

    barrier = pltpu.get_barrier_semaphore()

    def greet(i, _):
        pl.semaphore_signal(barrier, inc=1, device_id={"section": other(i)}, device_id_type=MESH)
        return 0

    lax.fori_loop(1, sections, greet, 0)
    for ring in (0, 1):
        for step in (1, -1):
            pl.semaphore_signal(
                barrier, inc=1, device_id={"mp": plane.peer(0, ring, step)}, device_id_type=MESH
            )

    half_features = features // 2
    loads = [
        pltpu.make_async_copy(
            head_hbm.at[:, pl.ds(t * half_features, half_features)], hbufs[t].at[mp], wsem.at[t]
        )
        for t in range(2)
    ]
    loads.append(pltpu.make_async_copy(w_in_hbm, w_in, wsem.at[2]))
    loads.append(pltpu.make_async_copy(w_out_hbm, w_out, wsem.at[3]))
    for load in loads:
        load.start()

    sub_id = lax.broadcasted_iota(jnp.int32, (rows, rows), 0)
    lane_id = lax.broadcasted_iota(jnp.int32, (rows, rows), 1)

    def line(values):
        return jnp.concatenate([values[0:1], values[1:2]], axis=1)

    def column(row):
        return jnp.sum(
            jnp.where(sub_id == lane_id, row.astype(F32), 0.0), axis=1, keepdims=True
        ).astype(jnp.int32)

    orow = line(matches_ref[...])
    ocol = column(orow)
    same = orow == ocol
    rank_col = jnp.sum(jnp.where(same & (lane_id < sub_id), 1.0, 0.0), axis=1, keepdims=True).astype(
        jnp.int32
    )
    rank_row = jnp.sum(jnp.where(same & (sub_id < lane_id), 1.0, 0.0), axis=0, keepdims=True).astype(
        jnp.int32
    )
    place = orow * cap + rank_row
    pick = jnp.where(
        lax.broadcasted_iota(jnp.int32, (agents * cap, rows), 0) == place, 1.0, 0.0
    ).astype(BF16)

    def send_off(step, seen):
        routed = jnp.dot(pick, seen.astype(BF16), preferred_element_type=F32).astype(BF16)
        zsends[step][...] = routed.reshape(agents, cap, width)

    view = jnp.concatenate([state_ref[:, 0, :], state_ref[:, 1, :]], axis=0)
    send_off(0, view)

    pl.semaphore_wait(barrier, sections - 1 + 4)

    def landing(step):
        return xbufs[step].at[mp, pl.ds(pl.multiple_of(me * cap, cap), cap), :]

    def route(step):
        def one(i, _):
            agent = other(i)
            pltpu.make_async_remote_copy(
                src_ref=zsends[step].at[agent],
                dst_ref=landing(step),
                send_sem=zsend_sem.at[step],
                recv_sem=zland_sem.at[step],
                device_id={"section": agent},
                device_id_type=MESH,
            ).start()
            return 0

        lax.fori_loop(1, sections, one, 0)
        pltpu.make_async_copy(zsends[step].at[me], landing(step), zland_sem.at[step]).start()

    def routed(step):
        whole = xbufs[step].at[mp]
        pltpu.make_async_copy(whole, whole, zland_sem.at[step]).wait()

    route(0)
    heads = [Gather(plane, hbufs[t], grsem.at[t], gssem.at[t]) for t in range(2)]
    inputs = [Gather(plane, xbufs[t], grsem.at[2 + t], gssem.at[2 + t]) for t in range(2)]
    loads[0].wait()
    for half in (0, 1):
        heads[0].own(half)

    act_now, act_next = column(line(actions_ref[0])), column(line(actions_ref[1]))
    act_other = jnp.concatenate([act_now[games:], act_now[:games]], axis=0)
    table = lax.broadcasted_iota(jnp.int32, (rows, embed_ref.shape[0]), 1)
    mix = jnp.where(table == act_now, 1.0, 0.0) + jnp.where(
        table == act_other, 0.5, 0.0
    )
    later = 0.8 * view + jnp.dot(mix.astype(BF16), embed_ref[...], preferred_element_type=F32)
    send_off(1, later)
    route(1)

    owner = jnp.where(lax.broadcasted_iota(jnp.int32, (agents, rows), 0) == orow, 1.0, 0.0)
    spot = lax.broadcasted_iota(jnp.int32, (rows, 128), 1)
    value = jnp.where(spot < cap, act_now, act_next)
    hit = (jnp.where(spot < cap, spot, spot - cap) == rank_col) & (spot < STEPS * cap)
    high = jnp.where(hit, value // 32, 0).astype(F32).astype(BF16)
    low = jnp.where(hit, value % 32, 0).astype(F32).astype(BF16)
    owner16 = owner.astype(BF16)
    named = 32.0 * jnp.dot(owner16, high, preferred_element_type=F32) + jnp.dot(
        owner16, low, preferred_element_type=F32
    )
    asend[...] = named.reshape(agents, 1, 128)

    def tell(i, _):
        agent = other(i)
        pltpu.make_async_remote_copy(
            src_ref=asend.at[agent],
            dst_ref=aland.at[lax.rem(me, per)],
            send_sem=asem.at[0],
            recv_sem=asem.at[1],
            device_id={"section": agent},
            device_id_type=MESH,
        ).start()
        return 0

    @pl.when(me // per == mp)
    def _():
        lax.fori_loop(1, sections, tell, 0)
        pltpu.make_async_copy(asend.at[me], aland.at[lax.rem(me, per)], asem.at[1]).start()

    def open_up(gather):
        for half in (0, 1):
            gather.first(half)
        for half in (0, 1):
            gather.pass_on(half, 0)
        for half in (0, 1):
            gather.second(half)

    def go_on(gather, k):
        for half in (0, 1):
            gather.pass_on(half, k)

    def close(gather):
        for half in (0, 1):
            for k in range(4):
                gather.last(half, k)

    open_up(heads[0])
    loads[1].wait()
    for half in (0, 1):
        heads[1].own(half)
    for k in (1, 2, 3):
        go_on(heads[0], k)
    routed(0)
    for half in (0, 1):
        inputs[0].own(half)
    open_up(heads[1])
    open_up(inputs[0])
    for k in (1, 2, 3):
        go_on(heads[1], k)
    routed(1)
    for half in (0, 1):
        inputs[1].own(half)
    for k in (1, 2, 3):
        go_on(inputs[0], k)
    loads[2].wait()
    loads[3].wait()
    open_up(inputs[1])

    each = agents * cap // chunks
    wide_cols = features // 2
    span = agents * cap // 2

    def project(t, half):
        lhs = jnp.concatenate([xbufs[t][i, half * span:(half + 1) * span, :] for i in range(chunks)], axis=1)
        total = jnp.dot(lhs, w_in[...], preferred_element_type=F32)
        wide = lhs.astype(F32)
        scale = lax.rsqrt(jnp.sum(wide * wide, axis=1, keepdims=True) * (1.0 / features) + EPS)
        hidden = jax.nn.gelu(total * scale).astype(BF16)
        hid[t, half * chunks // 2:(half + 1) * chunks // 2] = hidden.reshape(
            chunks // 2, each, hidden.shape[1]
        )

    outer = [
        [
            RingSum(
                plane, half, 0, part.at[2 * t + half], relay.at[2 * t + half], acc.at[2 * t + half],
                dst.at[2 * t + half], rs_s.at[2 * t + half], rs_r.at[2 * t + half],
            )
            for half in (0, 1)
        ]
        for t in range(2)
    ]
    inner = [
        [
            RingSum(
                plane, half, 1, sub.at[2 * t + half], srelay.at[2 * t + half], sacc.at[2 * t + half],
                sdst.at[2 * t + half], rs_s.at[4 + 2 * t + half], rs_r.at[4 + 2 * t + half],
            )
            for half in (0, 1)
        ]
        for t in range(2)
    ]

    def expand(t, half, k):
        if half == 0:
            index = [b * SIDE + wrap(plane.x, OFFS[k]) for b in range(SIDE)]
        else:
            index = [wrap(plane.y, OFFS[k]) * SIDE + b for b in range(SIDE)]
        lhs = jnp.concatenate([hid[t, i] for i in index], axis=0)
        total = jnp.dot(
            lhs, w_out[:, half * wide_cols:(half + 1) * wide_cols], preferred_element_type=F32
        )
        part[2 * t + half, k] = total.astype(BF16).reshape(SIDE, each, wide_cols)

    def spread_out(t):
        for half in (0, 1):
            expand(t, half, 3)
            outer[t][half].far()
        for half in (0, 1):
            expand(t, half, 1)
            expand(t, half, 2)
            outer[t][half].near()
        for half in (0, 1):
            expand(t, half, 0)

    def fold(t, half, k):
        b = wrap(plane.y if half == 0 else plane.x, OFFS[k])
        i = 2 * t + half
        return part[i, 0, b].astype(F32) + dst[i, 0, b].astype(F32) + dst[i, 1, b].astype(F32)

    def narrow(t):
        for half in (0, 1):
            i = 2 * t + half
            outer[t][half].arrive()
            sub[i, 3] = fold(t, half, 3).astype(BF16)
            inner[t][half].far()
            sub[i, 1] = fold(t, half, 1).astype(BF16)
            sub[i, 2] = fold(t, half, 2).astype(BF16)
            inner[t][half].near()
            keep[i] = fold(t, half, 0)

    def joined(rings):
        for half in (0, 1):
            rings[half].join()

    ident = lax.broadcasted_iota(jnp.int32, (cap, 128), 0) == lax.broadcasted_iota(
        jnp.int32, (cap, 128), 1
    )
    later_ident = lax.broadcasted_iota(jnp.int32, (cap, 128), 0) + cap == lax.broadcasted_iota(
        jnp.int32, (cap, 128), 1
    )

    def score(t):
        rest = []
        for half in (0, 1):
            i = 2 * t + half
            inner[t][half].arrive()
            rest.append(keep[i] + sdst[i, 0].astype(F32) + sdst[i, 1].astype(F32))
        mine = pl.ds(pl.multiple_of(mp * each, each), each)
        source = jnp.concatenate([xbufs[t][j, mine, :] for j in range(chunks)], axis=1).astype(F32)
        summed = source + jnp.concatenate(rest, axis=1)
        scale = lax.rsqrt(jnp.mean(summed * summed, axis=1, keepdims=True) + EPS)
        normed = (summed * scale).astype(BF16)
        scores = sum(
            lax.dot_general(
                normed[:, p * half_features:(p + 1) * half_features],
                hbufs[p][...].reshape(chunks * hbuf0.shape[1], half_features),
                (((1,), (1,)), ((), ())),
                preferred_element_type=F32,
            )
            for p in range(2)
        )
        peak = jnp.max(scores, axis=1, keepdims=True)
        total = jnp.sum(jnp.exp(scores - peak), axis=1, keepdims=True)
        eye = later_ident if t else ident
        chosen = jnp.concatenate(
            [jnp.sum(jnp.where(eye, aland[c], 0.0), axis=1, keepdims=True) for c in range(per)], axis=0
        )
        names = lax.broadcasted_iota(jnp.int32, scores.shape, 1)
        taken = jnp.sum(
            jnp.where(names == chosen.astype(jnp.int32), scores, 0.0), axis=1, keepdims=True
        )
        logp = taken - peak - jnp.log(total)
        for c in range(per):
            rsend[t, c] = jnp.sum(
                jnp.where(ident, logp[c * cap:(c + 1) * cap], 0.0), axis=0, keepdims=True
            )

    def give(t):
        def one(i, _):
            c = i // chunks
            dest = lax.rem(i, chunks)
            stays = (mp * per + c == me) & (dest == mp)

            @pl.when(jnp.logical_not(stays))
            def _():
                pltpu.make_async_remote_copy(
                    src_ref=rsend.at[t, c],
                    dst_ref=rland.at[t, me],
                    send_sem=bsend_sem.at[t],
                    recv_sem=bland_sem.at[t],
                    device_id={"section": mp * per + c, "mp": dest},
                    device_id_type=MESH,
                ).start()

            @pl.when(stays)
            def _():
                pltpu.make_async_copy(rsend.at[t, c], rland.at[t, me], bland_sem.at[t]).start()

            return 0

        lax.fori_loop(0, per * chunks, one, 0)

    def collect(t):
        land = rland.at[t]
        pltpu.make_async_copy(land, land, bland_sem.at[t]).wait()
        spread = lax.dot_general(
            rland[t].reshape(agents, 128), owner, (((0,), (0,)), ((), ())),
            precision=lax.Precision.HIGHEST, preferred_element_type=F32,
        )
        slot = lax.broadcasted_iota(jnp.int32, (128, rows), 0)
        value = jnp.sum(jnp.where(slot == rank_row, spread, 0.0), axis=0, keepdims=True)
        for player in range(2):
            out_ref[t, player:player + 1, :] = value[:, player * games:(player + 1) * games]

    close(inputs[0])
    project(0, 0)
    go_on(inputs[1], 1)
    project(0, 1)
    go_on(inputs[1], 2)
    go_on(inputs[1], 3)
    spread_out(0)
    close(inputs[1])
    project(1, 0)
    joined(outer[0])
    project(1, 1)
    spread_out(1)
    narrow(0)
    joined(outer[1])
    joined(inner[0])
    close(heads[0])
    close(heads[1])
    pltpu.make_async_copy(aland, aland, asem.at[1]).wait()
    score(0)
    give(0)
    narrow(1)
    joined(inner[1])
    score(1)
    give(1)
    collect(0)
    collect(1)

    for step in range(STEPS):
        full = zsends[step].at[pl.ds(0, sections - 1)]
        pltpu.make_async_copy(full, full, zsend_sem.at[step]).wait()

    @pl.when(me // per == mp)
    def _():
        told = asend.at[pl.ds(0, sections - 1)]
        pltpu.make_async_copy(told, told, asem.at[0]).wait()

    for t in range(2):
        heads[t].sent()
        inputs[t].sent()
        for half in (0, 1):
            outer[t][half].sent()
            inner[t][half].sent()
        given = rland.at[t, pl.ds(0, per * chunks - 1)]
        pltpu.make_async_copy(given, given, bsend_sem.at[t]).wait()

    @pl.when(me // per != mp)
    def _():
        for t in range(2):
            one = rland.at[t, 0]
            pltpu.make_async_copy(one, one, bsend_sem.at[t]).wait()


def per_device(matches, actions, state, embed, w_in, w_out, head):
    sections = lax.axis_size("section")
    games = matches.shape[0]
    width = state.shape[2]
    cap = 4 * games // sections
    served = sections * cap
    chunks = SIDE * SIDE
    each = served // chunks
    hidden = w_in.shape[3]
    features = w_in.shape[2]
    columns = head.shape[2]
    half_cols = features // 2
    vmem = pl.BlockSpec(memory_space=pltpu.VMEM)
    hbm = pl.BlockSpec(memory_space=pl.ANY)
    per = sections // chunks
    dma = pltpu.SemaphoreType.DMA
    out = pl.pallas_call(
        body,
        out_shape=jax.ShapeDtypeStruct((STEPS, 2, games), F32),
        in_specs=[vmem] * 4 + [hbm] * 3,
        out_specs=vmem,
        scratch_shapes=[
            pltpu.VMEM((sections, cap, width), BF16),
            pltpu.VMEM((sections, cap, width), BF16),
            pltpu.VMEM((sections, 1, 128), F32),
            pltpu.VMEM((per, 1, 128), F32),
            pltpu.VMEM((chunks, served, width), BF16),
            pltpu.VMEM((chunks, served, width), BF16),
            pltpu.VMEM((chunks, columns, half_cols), BF16),
            pltpu.VMEM((chunks, columns, half_cols), BF16),
            pltpu.VMEM((features, hidden), BF16),
            pltpu.VMEM((hidden, features), BF16),
            pltpu.VMEM((2, chunks, each, hidden), BF16),
            pltpu.VMEM((4, 4, SIDE, each, half_cols), BF16),
            pltpu.VMEM((4, 2, SIDE // 2, each, half_cols), BF16),
            pltpu.VMEM((4, 2, SIDE // 2, each, half_cols), BF16),
            pltpu.VMEM((4, 2, SIDE, each, half_cols), BF16),
            pltpu.VMEM((4, 4, each, half_cols), BF16),
            pltpu.VMEM((4, 2, each // 2, half_cols), BF16),
            pltpu.VMEM((4, 2, each // 2, half_cols), BF16),
            pltpu.VMEM((4, 2, each, half_cols), BF16),
            pltpu.VMEM((4, each, half_cols), F32),
            pltpu.VMEM((2, per, 1, 128), F32),
            pltpu.VMEM((2, sections, 1, 128), F32),
            dma((4,)), dma((2,)), dma((2,)), dma((2,)),
            dma((4, 40)), dma((4,)), dma((8,)), dma((8, 6)), dma((2,)), dma((2,)),
        ],
        compiler_params=pltpu.CompilerParams(
            collective_id=0, has_side_effects=True, vmem_limit_bytes=60 * 1024 * 1024
        ),
        name="league",
    )(matches.T, actions.swapaxes(1, 2), state, embed, w_in[0, 0], w_out[0, 0], head[0].T)
    return out.swapaxes(1, 2)


def solution(mesh):
    return jax.shard_map(
        per_device,
        mesh=mesh,
        in_specs=(
            P("section", None),
            P(None, "section", None),
            P("section", None, "mp"),
            P(None, "mp"),
            P("section", None, None, "mp"),
            P("section", None, "mp", None),
            P("section", None, "mp"),
        ),
        out_specs=P(None, "section", None),
        check_vma=False,
    )
```

```python
import jax
import jax.numpy as jnp
from jax import lax
from jax.experimental import pallas as pl
from jax.experimental.pallas import tpu as pltpu
from jax.sharding import PartitionSpec as P

STEPS = 2
SIDE = 4
EPS = 1e-06
MESH = pl.DeviceIdType.MESH
F32 = jnp.float32
BF16 = jnp.bfloat16

OFFS = (0, -1, 1, 2)


def wrap(pos, off):
    return lax.rem(pos + (off + SIDE), SIDE) if off else pos


class Plane:
    def __init__(self):
        self.mp = lax.axis_index("mp")
        self.y = self.mp // SIDE
        self.x = lax.rem(self.mp, SIDE)

    def at(self, half, da, db):
        if half == 0:
            return wrap(self.y, db) * SIDE + wrap(self.x, da)
        return wrap(self.y, da) * SIDE + wrap(self.x, db)

    def peer(self, half, ring, step):
        return self.at(half, step, 0) if ring == 0 else self.at(half, 0, step)


class Gather:
    def __init__(self, plane, buf, rsem, ssem):
        self.plane, self.buf, self.rsem, self.ssem = plane, buf, rsem, ssem
        self.rows = buf.shape[1]

    def copy(self, half, event, ring, step, da, db, part):
        quarter = self.rows // 4
        start = half * 2 * quarter + (quarter if part == 2 else 0)
        size = 2 * quarter if part == 0 else quarter
        ref = self.buf.at[self.plane.at(half, da, db), pl.ds(start, size), :]
        return pltpu.make_async_remote_copy(
            src_ref=ref,
            dst_ref=ref,
            send_sem=self.ssem,
            recv_sem=self.rsem.at[half * 20 + event],
            device_id={"mp": self.plane.peer(half, ring, step)},
            device_id_type=MESH,
        )

    def own(self, half):
        self.copy(half, 0, 0, 1, 0, 0, 0).start()
        self.copy(half, 1, 0, -1, 0, 0, 0).start()
        self.across(half, 0)

    def across(self, half, k):
        self.copy(half, 4 + 4 * k, 1, 1, OFFS[k], 0, 0).start()
        self.copy(half, 5 + 4 * k, 1, -1, OFFS[k], 0, 0).start()

    def first(self, half):
        self.copy(half, 0, 0, 1, -1, 0, 0).wait_recv()
        self.copy(half, 2, 0, 1, -1, 0, 1).start()
        self.across(half, 1)
        self.copy(half, 1, 0, -1, 1, 0, 0).wait_recv()
        self.copy(half, 3, 0, -1, 1, 0, 2).start()
        self.across(half, 2)

    def second(self, half):
        self.copy(half, 2, 0, 1, 2, 0, 1).wait_recv()
        self.copy(half, 3, 0, -1, 2, 0, 2).wait_recv()
        self.across(half, 3)

    def pass_on(self, half, k):
        self.copy(half, 4 + 4 * k, 1, 1, OFFS[k], -1, 0).wait_recv()
        self.copy(half, 6 + 4 * k, 1, 1, OFFS[k], -1, 1).start()
        self.copy(half, 5 + 4 * k, 1, -1, OFFS[k], 1, 0).wait_recv()
        self.copy(half, 7 + 4 * k, 1, -1, OFFS[k], 1, 2).start()

    def last(self, half, k):
        self.copy(half, 6 + 4 * k, 1, 1, OFFS[k], 2, 1).wait_recv()
        self.copy(half, 7 + 4 * k, 1, -1, OFFS[k], 2, 2).wait_recv()

    def sent(self):
        ref = self.buf.at[pl.ds(0, SIDE * SIDE - 1)]
        pltpu.make_async_copy(ref, ref, self.ssem).wait()


class RingSum:
    def __init__(self, plane, half, ring, src, relay, acc, dst, ssem, rsem):
        self.plane, self.half, self.ring = plane, half, ring
        self.src, self.relay, self.acc, self.dst = src, relay, acc, dst
        self.ssem, self.rsem = ssem, rsem
        self.cut = src.shape[1] // 2

    def copy(self, event):
        step = (1, -1)[event % 2]
        src, dst = self.src, self.dst
        lo, hi = pl.ds(0, self.cut), pl.ds(self.cut, self.cut)
        source, target = (
            lambda: (src.at[3, lo], self.relay.at[0]),
            lambda: (src.at[3, hi], self.relay.at[1]),
            lambda: (src.at[2, hi], dst.at[0, hi]),
            lambda: (src.at[1, lo], dst.at[1, lo]),
            lambda: (self.acc.at[0], dst.at[0, lo]),
            lambda: (self.acc.at[1], dst.at[1, hi]),
        )[event]()
        return pltpu.make_async_remote_copy(
            src_ref=source,
            dst_ref=target,
            send_sem=self.ssem,
            recv_sem=self.rsem.at[event],
            device_id={"mp": self.plane.peer(self.half, self.ring, step)},
            device_id_type=MESH,
        )

    def far(self):
        self.copy(0).start()
        self.copy(1).start()

    def near(self):
        self.copy(2).start()
        self.copy(3).start()

    def join(self):
        lo, hi = pl.ds(0, self.cut), pl.ds(self.cut, self.cut)
        self.copy(0).wait_recv()
        self.acc[0] = (self.src[2, lo].astype(F32) + self.relay[0].astype(F32)).astype(BF16)
        self.copy(4).start()
        self.copy(1).wait_recv()
        self.acc[1] = (self.src[1, hi].astype(F32) + self.relay[1].astype(F32)).astype(BF16)
        self.copy(5).start()

    def arrive(self):
        for event in range(2, 6):
            self.copy(event).wait_recv()

    def sent(self):
        ref = self.src.at[pl.ds(0, 3)]
        pltpu.make_async_copy(ref, ref, self.ssem).wait()


def body(
    matches_ref, actions_ref, state_ref, embed_ref, w_in_hbm, w_out_hbm, head_hbm,
    out_ref,
    zsend0, zsend1, asend, aland, xbuf0, xbuf1, hbuf0, hbuf1, w_in, w_out, hid,
    part, relay, acc, dst, sub, srelay, sacc, sdst, keep,
    rsend, rland,
    met, wsem, zsend_sem, zland_sem, asem, grsem, gssem, rs_s, rs_r, bsend_sem, bland_sem,
):
    plane = Plane()
    mp = plane.mp
    sections = lax.axis_size("section")
    me = lax.axis_index("section")
    games = matches_ref.shape[1]
    rows = 2 * games
    cap = zsend0.shape[1]
    agents = sections
    chunks = SIDE * SIDE
    per = sections // chunks
    zsends, xbufs, hbufs = (zsend0, zsend1), (xbuf0, xbuf1), (hbuf0, hbuf1)
    width = embed_ref.shape[1]
    features = width * chunks

    def other(i):
        k = sections - i
        odd, far = lax.rem(k, 2), (k + 1) // 2
        return lax.rem(me + odd * far + (1 - odd) * (sections - far), sections)

    column_z = sections // 2
    my_z, my_core = me // 2, lax.rem(me, 2)

    def along(off):
        return {"section": lax.rem(my_z + (off + column_z), column_z) * 2 + my_core}

    beside = {"section": my_z * 2 + 1 - my_core}
    barrier = pltpu.get_barrier_semaphore()
    close_by = [{"mp": plane.peer(0, ring, step)} for ring in (0, 1) for step in (1, -1)]
    close_by += [along(1), along(-1), beside]
    for device in close_by:
        pl.semaphore_signal(barrier, inc=1, device_id=device, device_id_type=MESH)

    def meet(stage, devices):
        for device in devices:
            pl.semaphore_signal(met.at[stage], inc=1, device_id=device, device_id_type=MESH)
        pl.semaphore_wait(met.at[stage], len(devices))

    half_features = features // 2
    loads = [
        pltpu.make_async_copy(
            head_hbm.at[:, pl.ds(t * half_features, half_features)], hbufs[t].at[mp], wsem.at[t]
        )
        for t in range(2)
    ]
    loads.append(pltpu.make_async_copy(w_in_hbm, w_in, wsem.at[2]))
    loads.append(pltpu.make_async_copy(w_out_hbm, w_out, wsem.at[3]))
    for load in loads:
        load.start()
    heads = [Gather(plane, hbufs[t], grsem.at[t], gssem.at[t]) for t in range(2)]
    inputs = [Gather(plane, xbufs[t], grsem.at[2 + t], gssem.at[2 + t]) for t in range(2)]
    pl.semaphore_wait(barrier, len(close_by))
    loads[0].wait()
    for half in (0, 1):
        heads[0].own(half)
    meet(0, [along(1), along(-1)])

    sub_id = lax.broadcasted_iota(jnp.int32, (rows, rows), 0)
    lane_id = lax.broadcasted_iota(jnp.int32, (rows, rows), 1)

    def line(values):
        return jnp.concatenate([values[0:1], values[1:2]], axis=1)

    def column(row):
        return jnp.sum(
            jnp.where(sub_id == lane_id, row.astype(F32), 0.0), axis=1, keepdims=True
        ).astype(jnp.int32)

    orow = line(matches_ref[...])
    ocol = column(orow)
    same = orow == ocol
    rank_col = jnp.sum(jnp.where(same & (lane_id < sub_id), 1.0, 0.0), axis=1, keepdims=True).astype(
        jnp.int32
    )
    rank_row = jnp.sum(jnp.where(same & (sub_id < lane_id), 1.0, 0.0), axis=0, keepdims=True).astype(
        jnp.int32
    )
    place = orow * cap + rank_row
    pick = jnp.where(
        lax.broadcasted_iota(jnp.int32, (agents * cap, rows), 0) == place, 1.0, 0.0
    ).astype(BF16)

    def send_off(step, seen):
        routed = jnp.dot(pick, seen.astype(BF16), preferred_element_type=F32).astype(BF16)
        zsends[step][...] = routed.reshape(agents, cap, width)

    view = jnp.concatenate([state_ref[:, 0, :], state_ref[:, 1, :]], axis=0)
    meet(1, [along(2), along(-2)])
    send_off(0, view)
    meet(2, [along(4), along(-4)])
    meet(3, [beside])

    def landing(step):
        return xbufs[step].at[mp, pl.ds(pl.multiple_of(me * cap, cap), cap), :]

    def route(step):
        def one(i, _):
            agent = other(i)
            pltpu.make_async_remote_copy(
                src_ref=zsends[step].at[agent],
                dst_ref=landing(step),
                send_sem=zsend_sem.at[step],
                recv_sem=zland_sem.at[step],
                device_id={"section": agent},
                device_id_type=MESH,
            ).start()
            return 0

        lax.fori_loop(1, sections, one, 0)
        pltpu.make_async_copy(zsends[step].at[me], landing(step), zland_sem.at[step]).start()

    def routed(step):
        whole = xbufs[step].at[mp]
        pltpu.make_async_copy(whole, whole, zland_sem.at[step]).wait()

    route(0)
    act_now, act_next = column(line(actions_ref[0])), column(line(actions_ref[1]))
    act_other = jnp.concatenate([act_now[games:], act_now[:games]], axis=0)
    table = lax.broadcasted_iota(jnp.int32, (rows, embed_ref.shape[0]), 1)
    mix = jnp.where(table == act_now, 1.0, 0.0) + jnp.where(
        table == act_other, 0.5, 0.0
    )
    later = 0.8 * view + jnp.dot(mix.astype(BF16), embed_ref[...], preferred_element_type=F32)
    send_off(1, later)
    route(1)

    owner = jnp.where(lax.broadcasted_iota(jnp.int32, (agents, rows), 0) == orow, 1.0, 0.0)
    spot = lax.broadcasted_iota(jnp.int32, (rows, 128), 1)
    value = jnp.where(spot < cap, act_now, act_next)
    hit = (jnp.where(spot < cap, spot, spot - cap) == rank_col) & (spot < STEPS * cap)
    high = jnp.where(hit, value // 32, 0).astype(F32).astype(BF16)
    low = jnp.where(hit, value % 32, 0).astype(F32).astype(BF16)
    owner16 = owner.astype(BF16)
    named = 32.0 * jnp.dot(owner16, high, preferred_element_type=F32) + jnp.dot(
        owner16, low, preferred_element_type=F32
    )
    asend[...] = named.reshape(agents, 1, 128)

    def tell(i, _):
        agent = other(i)
        pltpu.make_async_remote_copy(
            src_ref=asend.at[agent],
            dst_ref=aland.at[lax.rem(me, per)],
            send_sem=asem.at[0],
            recv_sem=asem.at[1],
            device_id={"section": agent},
            device_id_type=MESH,
        ).start()
        return 0

    @pl.when(me // per == mp)
    def _():
        lax.fori_loop(1, sections, tell, 0)
        pltpu.make_async_copy(asend.at[me], aland.at[lax.rem(me, per)], asem.at[1]).start()

    def open_up(gather):
        for half in (0, 1):
            gather.first(half)
        for half in (0, 1):
            gather.pass_on(half, 0)
        for half in (0, 1):
            gather.second(half)

    def go_on(gather, k):
        for half in (0, 1):
            gather.pass_on(half, k)

    def close(gather):
        for half in (0, 1):
            for k in range(4):
                gather.last(half, k)

    open_up(heads[0])
    loads[1].wait()
    for half in (0, 1):
        heads[1].own(half)
    for k in (1, 2, 3):
        go_on(heads[0], k)
    routed(0)
    for half in (0, 1):
        inputs[0].own(half)
    open_up(heads[1])
    routed(1)
    for half in (0, 1):
        inputs[1].own(half)
    open_up(inputs[0])
    open_up(inputs[1])
    for k in (1, 2, 3):
        go_on(inputs[0], k)
        go_on(inputs[1], k)
        go_on(heads[1], k)
    loads[2].wait()
    loads[3].wait()

    each = agents * cap // chunks
    wide_cols = features // 2
    span = agents * cap // 2

    def project(t, half):
        lhs = jnp.concatenate([xbufs[t][i, half * span:(half + 1) * span, :] for i in range(chunks)], axis=1)
        total = jnp.dot(lhs, w_in[...], preferred_element_type=F32)
        wide = lhs.astype(F32)
        scale = lax.rsqrt(jnp.sum(wide * wide, axis=1, keepdims=True) * (1.0 / features) + EPS)
        hidden = jax.nn.gelu(total * scale).astype(BF16)
        hid[t, half * chunks // 2:(half + 1) * chunks // 2] = hidden.reshape(
            chunks // 2, each, hidden.shape[1]
        )

    outer = [
        [
            RingSum(
                plane, half, 0, part.at[2 * t + half], relay.at[2 * t + half], acc.at[2 * t + half],
                dst.at[2 * t + half], rs_s.at[2 * t + half], rs_r.at[2 * t + half],
            )
            for half in (0, 1)
        ]
        for t in range(2)
    ]
    inner = [
        [
            RingSum(
                plane, half, 1, sub.at[2 * t + half], srelay.at[2 * t + half], sacc.at[2 * t + half],
                sdst.at[2 * t + half], rs_s.at[4 + 2 * t + half], rs_r.at[4 + 2 * t + half],
            )
            for half in (0, 1)
        ]
        for t in range(2)
    ]

    def expand(t, half, k):
        if half == 0:
            index = [b * SIDE + wrap(plane.x, OFFS[k]) for b in range(SIDE)]
        else:
            index = [wrap(plane.y, OFFS[k]) * SIDE + b for b in range(SIDE)]
        lhs = jnp.concatenate([hid[t, i] for i in index], axis=0)
        total = jnp.dot(
            lhs, w_out[:, half * wide_cols:(half + 1) * wide_cols], preferred_element_type=F32
        )
        part[2 * t + half, k] = total.astype(BF16).reshape(SIDE, each, wide_cols)

    def spread_out(t):
        for half in (0, 1):
            expand(t, half, 3)
            outer[t][half].far()
        for half in (0, 1):
            expand(t, half, 1)
            expand(t, half, 2)
            outer[t][half].near()
        for half in (0, 1):
            expand(t, half, 0)

    def fold(t, half, k):
        b = wrap(plane.y if half == 0 else plane.x, OFFS[k])
        i = 2 * t + half
        return part[i, 0, b].astype(F32) + dst[i, 0, b].astype(F32) + dst[i, 1, b].astype(F32)

    def narrow(t):
        for half in (0, 1):
            i = 2 * t + half
            outer[t][half].arrive()
            sub[i, 3] = fold(t, half, 3).astype(BF16)
            inner[t][half].far()
            sub[i, 1] = fold(t, half, 1).astype(BF16)
            sub[i, 2] = fold(t, half, 2).astype(BF16)
            inner[t][half].near()
            keep[i] = fold(t, half, 0)

    def joined(rings):
        for half in (0, 1):
            rings[half].join()

    ident = lax.broadcasted_iota(jnp.int32, (cap, 128), 0) == lax.broadcasted_iota(
        jnp.int32, (cap, 128), 1
    )
    later_ident = lax.broadcasted_iota(jnp.int32, (cap, 128), 0) + cap == lax.broadcasted_iota(
        jnp.int32, (cap, 128), 1
    )

    def score(t):
        rest = []
        for half in (0, 1):
            i = 2 * t + half
            inner[t][half].arrive()
            rest.append(keep[i] + sdst[i, 0].astype(F32) + sdst[i, 1].astype(F32))
        mine = pl.ds(pl.multiple_of(mp * each, each), each)
        source = jnp.concatenate([xbufs[t][j, mine, :] for j in range(chunks)], axis=1).astype(F32)
        summed = source + jnp.concatenate(rest, axis=1)
        scale = lax.rsqrt(jnp.mean(summed * summed, axis=1, keepdims=True) + EPS)
        normed = (summed * scale).astype(BF16)
        scores = sum(
            lax.dot_general(
                normed[:, p * half_features:(p + 1) * half_features],
                hbufs[p][...].reshape(chunks * hbuf0.shape[1], half_features),
                (((1,), (1,)), ((), ())),
                preferred_element_type=F32,
            )
            for p in range(2)
        )
        peak = jnp.max(scores, axis=1, keepdims=True)
        total = jnp.sum(jnp.exp(scores - peak), axis=1, keepdims=True)
        eye = later_ident if t else ident
        chosen = jnp.concatenate(
            [jnp.sum(jnp.where(eye, aland[c], 0.0), axis=1, keepdims=True) for c in range(per)], axis=0
        )
        names = lax.broadcasted_iota(jnp.int32, scores.shape, 1)
        taken = jnp.sum(
            jnp.where(names == chosen.astype(jnp.int32), scores, 0.0), axis=1, keepdims=True
        )
        logp = taken - peak - jnp.log(total)
        for c in range(per):
            rsend[t, c] = jnp.sum(
                jnp.where(ident, logp[c * cap:(c + 1) * cap], 0.0), axis=0, keepdims=True
            )

    def give(t):
        def one(i, _):
            c = i // chunks
            dest = lax.rem(i, chunks)
            stays = (mp * per + c == me) & (dest == mp)

            @pl.when(jnp.logical_not(stays))
            def _():
                pltpu.make_async_remote_copy(
                    src_ref=rsend.at[t, c],
                    dst_ref=rland.at[t, me],
                    send_sem=bsend_sem.at[t],
                    recv_sem=bland_sem.at[t],
                    device_id={"section": mp * per + c, "mp": dest},
                    device_id_type=MESH,
                ).start()

            @pl.when(stays)
            def _():
                pltpu.make_async_copy(rsend.at[t, c], rland.at[t, me], bland_sem.at[t]).start()

            return 0

        lax.fori_loop(0, per * chunks, one, 0)

    def collect(t):
        land = rland.at[t]
        pltpu.make_async_copy(land, land, bland_sem.at[t]).wait()
        spread = lax.dot_general(
            rland[t].reshape(agents, 128), owner, (((0,), (0,)), ((), ())),
            precision=lax.Precision.HIGHEST, preferred_element_type=F32,
        )
        slot = lax.broadcasted_iota(jnp.int32, (128, rows), 0)
        value = jnp.sum(jnp.where(slot == rank_row, spread, 0.0), axis=0, keepdims=True)
        for player in range(2):
            out_ref[t, player:player + 1, :] = value[:, player * games:(player + 1) * games]

    close(inputs[0])
    project(0, 0)
    project(0, 1)
    spread_out(0)
    close(inputs[1])
    project(1, 0)
    joined(outer[0])
    project(1, 1)
    spread_out(1)
    narrow(0)
    joined(outer[1])
    joined(inner[0])
    close(heads[0])
    close(heads[1])
    pltpu.make_async_copy(aland, aland, asem.at[1]).wait()
    score(0)
    give(0)
    narrow(1)
    joined(inner[1])
    score(1)
    give(1)
    collect(0)
    collect(1)

    for step in range(STEPS):
        full = zsends[step].at[pl.ds(0, sections - 1)]
        pltpu.make_async_copy(full, full, zsend_sem.at[step]).wait()

    @pl.when(me // per == mp)
    def _():
        told = asend.at[pl.ds(0, sections - 1)]
        pltpu.make_async_copy(told, told, asem.at[0]).wait()

    for t in range(2):
        heads[t].sent()
        inputs[t].sent()
        for half in (0, 1):
            outer[t][half].sent()
            inner[t][half].sent()
        given = rland.at[t, pl.ds(0, per * chunks - 1)]
        pltpu.make_async_copy(given, given, bsend_sem.at[t]).wait()

    @pl.when(me // per != mp)
    def _():
        for t in range(2):
            one = rland.at[t, 0]
            pltpu.make_async_copy(one, one, bsend_sem.at[t]).wait()


def per_device(matches, actions, state, embed, w_in, w_out, head):
    sections = lax.axis_size("section")
    games = matches.shape[0]
    width = state.shape[2]
    cap = 4 * games // sections
    served = sections * cap
    chunks = SIDE * SIDE
    each = served // chunks
    hidden = w_in.shape[3]
    features = w_in.shape[2]
    columns = head.shape[2]
    half_cols = features // 2
    vmem = pl.BlockSpec(memory_space=pltpu.VMEM)
    hbm = pl.BlockSpec(memory_space=pl.ANY)
    per = sections // chunks
    dma = pltpu.SemaphoreType.DMA
    out = pl.pallas_call(
        body,
        out_shape=jax.ShapeDtypeStruct((STEPS, 2, games), F32),
        in_specs=[vmem] * 4 + [hbm] * 3,
        out_specs=vmem,
        scratch_shapes=[
            pltpu.VMEM((sections, cap, width), BF16),
            pltpu.VMEM((sections, cap, width), BF16),
            pltpu.VMEM((sections, 1, 128), F32),
            pltpu.VMEM((per, 1, 128), F32),
            pltpu.VMEM((chunks, served, width), BF16),
            pltpu.VMEM((chunks, served, width), BF16),
            pltpu.VMEM((chunks, columns, half_cols), BF16),
            pltpu.VMEM((chunks, columns, half_cols), BF16),
            pltpu.VMEM((features, hidden), BF16),
            pltpu.VMEM((hidden, features), BF16),
            pltpu.VMEM((2, chunks, each, hidden), BF16),
            pltpu.VMEM((4, 4, SIDE, each, half_cols), BF16),
            pltpu.VMEM((4, 2, SIDE // 2, each, half_cols), BF16),
            pltpu.VMEM((4, 2, SIDE // 2, each, half_cols), BF16),
            pltpu.VMEM((4, 2, SIDE, each, half_cols), BF16),
            pltpu.VMEM((4, 4, each, half_cols), BF16),
            pltpu.VMEM((4, 2, each // 2, half_cols), BF16),
            pltpu.VMEM((4, 2, each // 2, half_cols), BF16),
            pltpu.VMEM((4, 2, each, half_cols), BF16),
            pltpu.VMEM((4, each, half_cols), F32),
            pltpu.VMEM((2, per, 1, 128), F32),
            pltpu.VMEM((2, sections, 1, 128), F32),
            pltpu.SemaphoreType.REGULAR((4,)),
            dma((4,)), dma((2,)), dma((2,)), dma((2,)),
            dma((4, 40)), dma((4,)), dma((8,)), dma((8, 6)), dma((2,)), dma((2,)),
        ],
        compiler_params=pltpu.CompilerParams(
            collective_id=0, has_side_effects=True, vmem_limit_bytes=60 * 1024 * 1024
        ),
        name="league",
    )(matches.T, actions.swapaxes(1, 2), state, embed, w_in[0, 0], w_out[0, 0], head[0].T)
    return out.swapaxes(1, 2)


def solution(mesh):
    return jax.shard_map(
        per_device,
        mesh=mesh,
        in_specs=(
            P("section", None),
            P(None, "section", None),
            P("section", None, "mp"),
            P(None, "mp"),
            P("section", None, None, "mp"),
            P("section", None, "mp", None),
            P("section", None, "mp"),
        ),
        out_specs=P(None, "section", None),
        check_vma=False,
    )
```

```python
import jax
import jax.numpy as jnp
from jax import lax
from jax.experimental import pallas as pl
from jax.experimental.pallas import tpu as pltpu
from jax.sharding import PartitionSpec as P

STEPS = 2
SIDE = 4
EPS = 1e-06
MESH = pl.DeviceIdType.MESH
F32 = jnp.float32
BF16 = jnp.bfloat16

OFFS = (0, -1, 1, 2)


def wrap(pos, off):
    return lax.rem(pos + (off + SIDE), SIDE) if off else pos


class Plane:
    def __init__(self):
        self.mp = lax.axis_index("mp")
        self.y = self.mp // SIDE
        self.x = lax.rem(self.mp, SIDE)

    def at(self, half, da, db):
        if half == 0:
            return wrap(self.y, db) * SIDE + wrap(self.x, da)
        return wrap(self.y, da) * SIDE + wrap(self.x, db)

    def peer(self, half, ring, step):
        return self.at(half, step, 0) if ring == 0 else self.at(half, 0, step)


class Gather:
    def __init__(self, plane, buf, rsem, ssem):
        self.plane, self.buf, self.rsem, self.ssem = plane, buf, rsem, ssem
        self.rows = buf.shape[1]

    def copy(self, half, event, ring, step, da, db, part):
        quarter = self.rows // 4
        start = half * 2 * quarter + (quarter if part == 2 else 0)
        size = 2 * quarter if part == 0 else quarter
        ref = self.buf.at[self.plane.at(half, da, db), pl.ds(start, size), :]
        return pltpu.make_async_remote_copy(
            src_ref=ref,
            dst_ref=ref,
            send_sem=self.ssem,
            recv_sem=self.rsem.at[half * 20 + event],
            device_id={"mp": self.plane.peer(half, ring, step)},
            device_id_type=MESH,
        )

    def own(self, half):
        self.copy(half, 0, 0, 1, 0, 0, 0).start()
        self.copy(half, 1, 0, -1, 0, 0, 0).start()
        self.across(half, 0)

    def across(self, half, k):
        self.copy(half, 4 + 4 * k, 1, 1, OFFS[k], 0, 0).start()
        self.copy(half, 5 + 4 * k, 1, -1, OFFS[k], 0, 0).start()

    def first(self, half):
        self.copy(half, 0, 0, 1, -1, 0, 0).wait_recv()
        self.copy(half, 2, 0, 1, -1, 0, 1).start()
        self.across(half, 1)
        self.copy(half, 1, 0, -1, 1, 0, 0).wait_recv()
        self.copy(half, 3, 0, -1, 1, 0, 2).start()
        self.across(half, 2)

    def second(self, half):
        self.copy(half, 2, 0, 1, 2, 0, 1).wait_recv()
        self.copy(half, 3, 0, -1, 2, 0, 2).wait_recv()
        self.across(half, 3)

    def pass_on(self, half, k):
        self.copy(half, 4 + 4 * k, 1, 1, OFFS[k], -1, 0).wait_recv()
        self.copy(half, 6 + 4 * k, 1, 1, OFFS[k], -1, 1).start()
        self.copy(half, 5 + 4 * k, 1, -1, OFFS[k], 1, 0).wait_recv()
        self.copy(half, 7 + 4 * k, 1, -1, OFFS[k], 1, 2).start()

    def last(self, half, k):
        self.copy(half, 6 + 4 * k, 1, 1, OFFS[k], 2, 1).wait_recv()
        self.copy(half, 7 + 4 * k, 1, -1, OFFS[k], 2, 2).wait_recv()

    def sent(self):
        ref = self.buf.at[pl.ds(0, SIDE * SIDE - 1)]
        pltpu.make_async_copy(ref, ref, self.ssem).wait()


class RingSum:
    def __init__(self, plane, half, ring, src, relay, acc, dst, ssem, rsem):
        self.plane, self.half, self.ring = plane, half, ring
        self.src, self.relay, self.acc, self.dst = src, relay, acc, dst
        self.ssem, self.rsem = ssem, rsem
        self.cut = src.shape[1] // 2

    def copy(self, event):
        step = (1, -1)[event % 2]
        src, dst = self.src, self.dst
        lo, hi = pl.ds(0, self.cut), pl.ds(self.cut, self.cut)
        source, target = (
            lambda: (src.at[3, lo], self.relay.at[0]),
            lambda: (src.at[3, hi], self.relay.at[1]),
            lambda: (src.at[2, hi], dst.at[0, hi]),
            lambda: (src.at[1, lo], dst.at[1, lo]),
            lambda: (self.acc.at[0], dst.at[0, lo]),
            lambda: (self.acc.at[1], dst.at[1, hi]),
        )[event]()
        return pltpu.make_async_remote_copy(
            src_ref=source,
            dst_ref=target,
            send_sem=self.ssem,
            recv_sem=self.rsem.at[event],
            device_id={"mp": self.plane.peer(self.half, self.ring, step)},
            device_id_type=MESH,
        )

    def far(self):
        self.copy(0).start()
        self.copy(1).start()

    def near(self):
        self.copy(2).start()
        self.copy(3).start()

    def join(self):
        lo, hi = pl.ds(0, self.cut), pl.ds(self.cut, self.cut)
        self.copy(0).wait_recv()
        self.acc[0] = (self.src[2, lo].astype(F32) + self.relay[0].astype(F32)).astype(BF16)
        self.copy(4).start()
        self.copy(1).wait_recv()
        self.acc[1] = (self.src[1, hi].astype(F32) + self.relay[1].astype(F32)).astype(BF16)
        self.copy(5).start()

    def arrive(self):
        for event in range(2, 6):
            self.copy(event).wait_recv()

    def sent(self):
        ref = self.src.at[pl.ds(0, 3)]
        pltpu.make_async_copy(ref, ref, self.ssem).wait()


def body(
    matches_ref, actions_ref, state_ref, embed_ref, w_in_hbm, w_out_hbm, head_hbm,
    out_ref,
    zsend0, zsend1, asend, aland, xbuf0, xbuf1, hown, hbuf, w_in, w_out, hid,
    part, relay, acc, dst, sub, srelay, sacc, sdst, keep,
    raw, lsub, lrelay, lacc, ldst, ssend, sland,
    rsend, rland,
    wsem, zsend_sem, zland_sem, asem, hsem, hssem, grsem, gssem, rs_s, rs_r, sq_s, sq_r, bsem,
):
    plane = Plane()
    mp = plane.mp
    sections = lax.axis_size("section")
    me = lax.axis_index("section")
    games = matches_ref.shape[1]
    rows = 2 * games
    cap = zsend0.shape[1]
    agents = sections
    chunks = SIDE * SIDE
    per = sections // chunks
    zsends, xbufs = (zsend0, zsend1), (xbuf0, xbuf1)
    turn = plane.x * SIDE + plane.y
    width = embed_ref.shape[1]
    features = width * chunks

    def other(i):
        k = sections - i
        odd, far = lax.rem(k, 2), (k + 1) // 2
        return lax.rem(me + odd * far + (1 - odd) * (sections - far), sections)

    barrier = pltpu.get_barrier_semaphore()

    def greet(i, _):
        pl.semaphore_signal(barrier, inc=1, device_id={"section": other(i)}, device_id_type=MESH)
        return 0

    lax.fori_loop(1, sections, greet, 0)
    for ring in (0, 1):
        for step in (1, -1):
            pl.semaphore_signal(
                barrier, inc=1, device_id={"mp": plane.peer(0, ring, step)}, device_id_type=MESH
            )
    pl.semaphore_signal(barrier, inc=1, device_id={"mp": plane.peer(0, 1, 2)}, device_id_type=MESH)

    quarter = features // SIDE
    loads = [
        pltpu.make_async_copy(head_hbm.at[:, pl.ds(f * quarter, quarter)], hown.at[f], wsem.at[f])
        for f in range(SIDE)
    ]
    loads.append(pltpu.make_async_copy(w_in_hbm, w_in, wsem.at[SIDE]))
    loads.append(pltpu.make_async_copy(w_out_hbm, w_out, wsem.at[SIDE + 1]))
    for load in loads:
        load.start()

    sub_id = lax.broadcasted_iota(jnp.int32, (rows, rows), 0)
    lane_id = lax.broadcasted_iota(jnp.int32, (rows, rows), 1)

    def line(values):
        return jnp.concatenate([values[0:1], values[1:2]], axis=1)

    def column(row):
        return jnp.sum(
            jnp.where(sub_id == lane_id, row.astype(F32), 0.0), axis=1, keepdims=True
        ).astype(jnp.int32)

    orow = line(matches_ref[...])
    ocol = column(orow)
    same = orow == ocol
    rank_col = jnp.sum(jnp.where(same & (lane_id < sub_id), 1.0, 0.0), axis=1, keepdims=True).astype(
        jnp.int32
    )
    rank_row = jnp.sum(jnp.where(same & (sub_id < lane_id), 1.0, 0.0), axis=0, keepdims=True).astype(
        jnp.int32
    )
    place = orow * cap + rank_row
    pick = jnp.where(
        lax.broadcasted_iota(jnp.int32, (agents * cap, rows), 0) == place, 1.0, 0.0
    ).astype(BF16)

    def send_off(step, seen):
        routed = jnp.dot(pick, seen.astype(BF16), preferred_element_type=F32).astype(BF16)
        zsends[step][...] = routed.reshape(agents, cap, width)

    view = jnp.concatenate([state_ref[:, 0, :], state_ref[:, 1, :]], axis=0)
    send_off(0, view)

    pl.semaphore_wait(barrier, sections - 1 + 5)

    def landing(step):
        return xbufs[step].at[mp, pl.ds(pl.multiple_of(me * cap, cap), cap), :]

    def route(step):
        def one(i, _):
            agent = other(i)
            pltpu.make_async_remote_copy(
                src_ref=zsends[step].at[agent],
                dst_ref=landing(step),
                send_sem=zsend_sem.at[step],
                recv_sem=zland_sem.at[step],
                device_id={"section": agent},
                device_id_type=MESH,
            ).start()
            return 0

        lax.fori_loop(1, sections, one, 0)
        pltpu.make_async_copy(zsends[step].at[me], landing(step), zland_sem.at[step]).start()

    def routed(step):
        whole = xbufs[step].at[mp]
        pltpu.make_async_copy(whole, whole, zland_sem.at[step]).wait()

    route(0)
    inputs = [Gather(plane, xbufs[t], grsem.at[t], gssem.at[t]) for t in range(2)]
    for f in range(SIDE):
        loads[f].wait()

    def deal(d):
        return pltpu.make_async_remote_copy(
            src_ref=hown.at[wrap(plane.y, d)],
            dst_ref=hbuf.at[plane.y, plane.x],
            send_sem=hssem.at[0],
            recv_sem=hsem.at[d],
            device_id={"mp": wrap(plane.y, d) * SIDE + plane.x},
            device_id_type=MESH,
        )

    def share(event, step, off, start, size):
        ref = hbuf.at[pl.ds(start, size), wrap(plane.x, off)]
        return pltpu.make_async_remote_copy(
            src_ref=ref,
            dst_ref=ref,
            send_sem=hssem.at[1],
            recv_sem=hsem.at[4 + event],
            device_id={"mp": plane.y * SIDE + wrap(plane.x, step)},
            device_id_type=MESH,
        )

    for d in (1, 2, 3):
        deal(d).start()
    own_head = pltpu.make_async_copy(hown.at[plane.y], hbuf.at[plane.y, plane.x], hsem.at[0])
    own_head.start()

    act_now, act_next = column(line(actions_ref[0])), column(line(actions_ref[1]))
    act_other = jnp.concatenate([act_now[games:], act_now[:games]], axis=0)
    table = lax.broadcasted_iota(jnp.int32, (rows, embed_ref.shape[0]), 1)
    mix = jnp.where(table == act_now, 1.0, 0.0) + jnp.where(
        table == act_other, 0.5, 0.0
    )
    later = 0.8 * view + jnp.dot(mix.astype(BF16), embed_ref[...], preferred_element_type=F32)
    send_off(1, later)
    route(1)

    owner = jnp.where(lax.broadcasted_iota(jnp.int32, (agents, rows), 0) == orow, 1.0, 0.0)
    spot = lax.broadcasted_iota(jnp.int32, (rows, 128), 1)
    value = jnp.where(spot < cap, act_now, act_next)
    hit = (jnp.where(spot < cap, spot, spot - cap) == rank_col) & (spot < STEPS * cap)
    high = jnp.where(hit, value // 32, 0).astype(F32).astype(BF16)
    low = jnp.where(hit, value % 32, 0).astype(F32).astype(BF16)
    owner16 = owner.astype(BF16)
    named = 32.0 * jnp.dot(owner16, high, preferred_element_type=F32) + jnp.dot(
        owner16, low, preferred_element_type=F32
    )
    asend[...] = named.reshape(agents, 1, 128)

    def tell(i, _):
        agent = other(i)
        pltpu.make_async_remote_copy(
            src_ref=asend.at[agent],
            dst_ref=aland.at[lax.rem(me, per)],
            send_sem=asem.at[0],
            recv_sem=asem.at[1],
            device_id={"section": agent},
            device_id_type=MESH,
        ).start()
        return 0

    @pl.when(me // per == turn)
    def _():
        lax.fori_loop(1, sections, tell, 0)
        pltpu.make_async_copy(asend.at[me], aland.at[lax.rem(me, per)], asem.at[1]).start()

    def open_up(gather):
        for half in (0, 1):
            gather.first(half)
        for half in (0, 1):
            gather.pass_on(half, 0)
        for half in (0, 1):
            gather.second(half)

    def go_on(gather, k):
        for half in (0, 1):
            gather.pass_on(half, k)

    def close(gather):
        for half in (0, 1):
            for k in range(4):
                gather.last(half, k)

    own_head.wait()
    for d in (1, 2, 3):
        deal(d).wait_recv()
    share(0, 1, 0, 0, SIDE).start()
    share(1, -1, 0, 0, SIDE).start()
    routed(0)
    for half in (0, 1):
        inputs[0].own(half)
    share(0, 1, -1, 0, SIDE).wait_recv()
    share(2, 1, -1, 0, SIDE // 2).start()
    share(1, -1, 1, 0, SIDE).wait_recv()
    share(3, -1, 1, SIDE // 2, SIDE // 2).start()
    for half in (0, 1):
        inputs[0].first(half)
    for half in (0, 1):
        inputs[0].pass_on(half, 0)
    routed(1)
    for half in (0, 1):
        inputs[1].own(half)
    for half in (0, 1):
        inputs[0].second(half)
    open_up(inputs[1])
    for k in (1, 2, 3):
        go_on(inputs[0], k)
        go_on(inputs[1], k)
    loads[SIDE].wait()
    loads[SIDE + 1].wait()

    each = agents * cap // chunks
    span = agents * cap // 2

    def project(t, half):
        lhs = jnp.concatenate([xbufs[t][i, half * span:(half + 1) * span, :] for i in range(chunks)], axis=1)
        total = jnp.dot(lhs, w_in[...], preferred_element_type=F32)
        wide = lhs.astype(F32)
        scale = lax.rsqrt(jnp.sum(wide * wide, axis=1, keepdims=True) * (1.0 / features) + EPS)
        hidden = jax.nn.gelu(total * scale).astype(BF16)
        hid[t, half * chunks // 2:(half + 1) * chunks // 2] = hidden.reshape(
            chunks // 2, each, hidden.shape[1]
        )

    outer = [
        [
            RingSum(
                plane, half, 0, part.at[2 * t + half], relay.at[2 * t + half], acc.at[2 * t + half],
                dst.at[2 * t + half], rs_s.at[2 * t + half], rs_r.at[2 * t + half],
            )
            for half in (0, 1)
        ]
        for t in range(2)
    ]
    inner = [
        [
            RingSum(
                plane, half, 1, sub.at[2 * t + half], srelay.at[2 * t + half], sacc.at[2 * t + half],
                sdst.at[2 * t + half], rs_s.at[4 + 2 * t + half], rs_r.at[4 + 2 * t + half],
            )
            for half in (0, 1)
        ]
        for t in range(2)
    ]

    def nearness(place, pos):
        d = lax.rem(place + SIDE - pos, SIDE)
        return (lax.rem(d, 3) + 1) * jnp.minimum(d, 1)

    def expand(t, half):
        pair = [c * SIDE + 2 * half + b for c in range(SIDE) for b in range(2)]
        lhs = jnp.concatenate([hid[t, i] for i in pair], axis=0)
        total = jnp.dot(lhs, w_out[...], preferred_element_type=F32).astype(BF16)
        for c in range(SIDE):
            for f in range(SIDE):
                piece = total[c * 2 * each:(c + 1) * 2 * each, f * quarter:(f + 1) * quarter]
                if half == 0:
                    part[2 * t + half, nearness(c, plane.x), f] = piece
                else:
                    part[2 * t + half, nearness(f, plane.y), c] = piece

    def spread_out(t):
        for half in (0, 1):
            expand(t, half)
            outer[t][half].far()
            outer[t][half].near()

    def fold(t, half, k):
        b = wrap(plane.y if half == 0 else plane.x, OFFS[k])
        i = 2 * t + half
        return part[i, 0, b].astype(F32) + dst[i, 0, b].astype(F32) + dst[i, 1, b].astype(F32)

    def narrow(t):
        for half in (0, 1):
            i = 2 * t + half
            outer[t][half].arrive()
            sub[i, 3] = fold(t, half, 3).astype(BF16)
            inner[t][half].far()
            sub[i, 1] = fold(t, half, 1).astype(BF16)
            sub[i, 2] = fold(t, half, 2).astype(BF16)
            inner[t][half].near()
            keep[i] = fold(t, half, 0)

    def joined(rings):
        for half in (0, 1):
            rings[half].join()

    ident = lax.broadcasted_iota(jnp.int32, (cap, 128), 0) == lax.broadcasted_iota(
        jnp.int32, (cap, 128), 1
    )
    later_ident = lax.broadcasted_iota(jnp.int32, (cap, 128), 0) + cap == lax.broadcasted_iota(
        jnp.int32, (cap, 128), 1
    )

    logit_sums = [
        RingSum(
            plane, 0, 1, lsub.at[t], lrelay.at[t], lacc.at[t], ldst.at[t], rs_s.at[8 + t], rs_r.at[8 + t]
        )
        for t in range(2)
    ]
    strip = SIDE * each
    diagonal = lax.broadcasted_iota(jnp.int32, (strip, strip), 0) == lax.broadcasted_iota(
        jnp.int32, (strip, strip), 1
    )

    def square_copy(t, d):
        return pltpu.make_async_remote_copy(
            src_ref=ssend.at[t],
            dst_ref=sland.at[t, d - 1],
            send_sem=sq_s.at[t],
            recv_sem=sq_r.at[3 * t + d - 1],
            device_id={"mp": wrap(plane.y, d) * SIDE + plane.x},
            device_id_type=MESH,
        )

    def half_score(t):
        rest = []
        for half in (0, 1):
            i = 2 * t + half
            inner[t][half].arrive()
            rest.append(keep[i] + sdst[i, 0].astype(F32) + sdst[i, 1].astype(F32))
        mine = pl.ds(pl.multiple_of(plane.x * strip, strip), strip)
        source = jnp.concatenate(
            [xbufs[t][plane.y * SIDE + j, mine, :] for j in range(SIDE)], axis=1
        ).astype(F32)
        summed = source + jnp.concatenate(rest, axis=0)
        squares = jnp.sum(summed * summed, axis=1, keepdims=True)
        ssend[t] = jnp.sum(jnp.where(diagonal, squares, 0.0), axis=0, keepdims=True)
        for d in (1, 2, 3):
            square_copy(t, d).start()
        scores = lax.dot_general(
            summed.astype(BF16),
            hbuf[...].reshape(chunks * hbuf.shape[2], quarter),
            (((1,), (1,)), ((), ())),
            preferred_element_type=F32,
        )
        raw[t] = scores.reshape(SIDE, each, scores.shape[1])
        for k in (1, 2, 3):
            lsub[t, k] = raw[t, wrap(plane.y, OFFS[k])].astype(BF16)
        logit_sums[t].far()
        logit_sums[t].near()

    def score(t):
        logit_sums[t].arrive()
        for d in (1, 2, 3):
            square_copy(t, d).wait_recv()
        row = ssend[t] + sland[t, 0] + sland[t, 1] + sland[t, 2]
        at_row = lax.broadcasted_iota(jnp.int32, (each, strip), 1) == (
            lax.broadcasted_iota(jnp.int32, (each, strip), 0) + plane.y * each
        )
        squares = jnp.sum(jnp.where(at_row, row, 0.0), axis=1, keepdims=True)
        scale = lax.rsqrt(squares * (1.0 / features) + EPS)
        scores = scale * (raw[t, plane.y] + ldst[t, 0].astype(F32) + ldst[t, 1].astype(F32))
        peak = jnp.max(scores, axis=1, keepdims=True)
        total = jnp.sum(jnp.exp(scores - peak), axis=1, keepdims=True)
        eye = later_ident if t else ident
        chosen = jnp.concatenate(
            [jnp.sum(jnp.where(eye, aland[c], 0.0), axis=1, keepdims=True) for c in range(per)], axis=0
        )
        names = lax.broadcasted_iota(jnp.int32, scores.shape, 1)
        taken = jnp.sum(
            jnp.where(names == chosen.astype(jnp.int32), scores, 0.0), axis=1, keepdims=True
        )
        logp = taken - peak - jnp.log(total)
        return [
            jnp.sum(jnp.where(eye, logp[c * cap:(c + 1) * cap], 0.0), axis=0, keepdims=True)
            for c in range(per)
        ]

    def give(i, _):
        c = i // chunks
        dest = lax.rem(i, chunks)
        stays = (turn * per + c == me) & (dest == mp)

        @pl.when(jnp.logical_not(stays))
        def _():
            pltpu.make_async_remote_copy(
                src_ref=rsend.at[c],
                dst_ref=rland.at[me],
                send_sem=bsem.at[0],
                recv_sem=bsem.at[1],
                device_id={"section": turn * per + c, "mp": dest},
                device_id_type=MESH,
            ).start()

        @pl.when(stays)
        def _():
            pltpu.make_async_copy(rsend.at[c], rland.at[me], bsem.at[1]).start()

        return 0

    close(inputs[0])
    project(0, 0)
    project(0, 1)
    spread_out(0)
    close(inputs[1])
    project(1, 0)
    joined(outer[0])
    project(1, 1)
    spread_out(1)
    joined(outer[1])
    narrow(0)
    joined(inner[0])
    narrow(1)
    joined(inner[1])
    share(2, 1, 2, 0, SIDE // 2).wait_recv()
    share(3, -1, 2, SIDE // 2, SIDE // 2).wait_recv()
    half_score(0)
    half_score(1)
    joined(logit_sums)
    pltpu.make_async_copy(aland, aland, asem.at[1]).wait()
    found = [score(t) for t in range(2)]
    for c in range(per):
        rsend[c] = found[0][c] + found[1][c]
    lax.fori_loop(0, per * chunks, give, 0)
    pltpu.make_async_copy(rland, rland, bsem.at[1]).wait()
    spread = lax.dot_general(
        rland[...].reshape(agents, 128), owner, (((0,), (0,)), ((), ())),
        precision=lax.Precision.HIGHEST, preferred_element_type=F32,
    )
    slot = lax.broadcasted_iota(jnp.int32, (128, rows), 0)
    for t in range(STEPS):
        value = jnp.sum(jnp.where(slot == rank_row + t * cap, spread, 0.0), axis=0, keepdims=True)
        for player in range(2):
            out_ref[t, player:player + 1, :] = value[:, player * games:(player + 1) * games]

    for step in range(STEPS):
        full = zsends[step].at[pl.ds(0, sections - 1)]
        pltpu.make_async_copy(full, full, zsend_sem.at[step]).wait()

    @pl.when(me // per == turn)
    def _():
        told = asend.at[pl.ds(0, sections - 1)]
        pltpu.make_async_copy(told, told, asem.at[0]).wait()

    dealt = hown.at[pl.ds(0, 3)]
    pltpu.make_async_copy(dealt, dealt, hssem.at[0]).wait()
    shared = hbuf.at[pl.ds(0, 3)]
    pltpu.make_async_copy(shared, shared, hssem.at[1]).wait()
    for t in range(2):
        inputs[t].sent()
        for half in (0, 1):
            outer[t][half].sent()
            inner[t][half].sent()
        logit_sums[t].sent()
        told = sland.at[t]
        pltpu.make_async_copy(told, told, sq_s.at[t]).wait()
    given = rland.at[pl.ds(0, per * chunks - 1)]
    pltpu.make_async_copy(given, given, bsem.at[0]).wait()

    @pl.when(me // per != turn)
    def _():
        one = rland.at[0]
        pltpu.make_async_copy(one, one, bsem.at[0]).wait()


def per_device(matches, actions, state, embed, w_in, w_out, head):
    sections = lax.axis_size("section")
    games = matches.shape[0]
    width = state.shape[2]
    cap = 4 * games // sections
    served = sections * cap
    chunks = SIDE * SIDE
    each = served // chunks
    hidden = w_in.shape[3]
    features = w_in.shape[2]
    columns = head.shape[2]
    quarter = features // SIDE
    actions_all = columns * chunks
    vmem = pl.BlockSpec(memory_space=pltpu.VMEM)
    hbm = pl.BlockSpec(memory_space=pl.ANY)
    per = sections // chunks
    dma = pltpu.SemaphoreType.DMA
    out = pl.pallas_call(
        body,
        out_shape=jax.ShapeDtypeStruct((STEPS, 2, games), F32),
        in_specs=[vmem] * 4 + [hbm] * 3,
        out_specs=vmem,
        scratch_shapes=[
            pltpu.VMEM((sections, cap, width), BF16),
            pltpu.VMEM((sections, cap, width), BF16),
            pltpu.VMEM((sections, 1, 128), F32),
            pltpu.VMEM((per, 1, 128), F32),
            pltpu.VMEM((chunks, served, width), BF16),
            pltpu.VMEM((chunks, served, width), BF16),
            pltpu.VMEM((SIDE, columns, quarter), BF16),
            pltpu.VMEM((SIDE, SIDE, columns, quarter), BF16),
            pltpu.VMEM((features, hidden), BF16),
            pltpu.VMEM((hidden, features), BF16),
            pltpu.VMEM((2, chunks, each, hidden), BF16),
            pltpu.VMEM((4, 4, SIDE, 2 * each, quarter), BF16),
            pltpu.VMEM((4, 2, SIDE // 2, 2 * each, quarter), BF16),
            pltpu.VMEM((4, 2, SIDE // 2, 2 * each, quarter), BF16),
            pltpu.VMEM((4, 2, SIDE, 2 * each, quarter), BF16),
            pltpu.VMEM((4, 4, 2 * each, quarter), BF16),
            pltpu.VMEM((4, 2, each, quarter), BF16),
            pltpu.VMEM((4, 2, each, quarter), BF16),
            pltpu.VMEM((4, 2, 2 * each, quarter), BF16),
            pltpu.VMEM((4, 2 * each, quarter), F32),
            pltpu.VMEM((2, SIDE, each, actions_all), F32),
            pltpu.VMEM((2, 4, each, actions_all), BF16),
            pltpu.VMEM((2, 2, each // 2, actions_all), BF16),
            pltpu.VMEM((2, 2, each // 2, actions_all), BF16),
            pltpu.VMEM((2, 2, each, actions_all), BF16),
            pltpu.VMEM((2, 1, SIDE * each), F32),
            pltpu.VMEM((2, 3, 1, SIDE * each), F32),
            pltpu.VMEM((per, 1, 128), F32),
            pltpu.VMEM((sections, 1, 128), F32),
            dma((6,)), dma((2,)), dma((2,)), dma((2,)), dma((8,)), dma((2,)),
            dma((2, 40)), dma((2,)), dma((10,)), dma((10, 6)), dma((2,)), dma((6,)), dma((2,)),
        ],
        compiler_params=pltpu.CompilerParams(
            collective_id=0, has_side_effects=True, vmem_limit_bytes=60 * 1024 * 1024
        ),
        name="league",
    )(matches.T, actions.swapaxes(1, 2), state, embed, w_in[0, 0], w_out[0, 0], head[0].T)
    return out.swapaxes(1, 2)


def solution(mesh):
    return jax.shard_map(
        per_device,
        mesh=mesh,
        in_specs=(
            P("section", None),
            P(None, "section", None),
            P("section", None, "mp"),
            P(None, "mp"),
            P("section", None, None, "mp"),
            P("section", None, "mp", None),
            P("section", None, "mp"),
        ),
        out_specs=P(None, "section", None),
        check_vma=False,
    )
```

```python
import jax
import jax.numpy as jnp
from jax import lax
from jax.experimental import pallas as pl
from jax.experimental.pallas import tpu as pltpu
from jax.sharding import PartitionSpec as P

STEPS = 2
SIDE = 4
EPS = 1e-06
MESH = pl.DeviceIdType.MESH
F32 = jnp.float32
BF16 = jnp.bfloat16

OFFS = (0, -1, 1, 2)


def wrap(pos, off):
    return lax.rem(pos + (off + SIDE), SIDE) if off else pos


class Plane:
    def __init__(self):
        self.mp = lax.axis_index("mp")
        self.y = self.mp // SIDE
        self.x = lax.rem(self.mp, SIDE)

    def at(self, half, da, db):
        if half == 0:
            return wrap(self.y, db) * SIDE + wrap(self.x, da)
        return wrap(self.y, da) * SIDE + wrap(self.x, db)

    def peer(self, half, ring, step):
        return self.at(half, step, 0) if ring == 0 else self.at(half, 0, step)


class Gather:
    def __init__(self, plane, buf, rsem, ssem):
        self.plane, self.buf, self.rsem, self.ssem = plane, buf, rsem, ssem
        self.rows = buf.shape[1]

    def copy(self, half, event, ring, step, da, db, part):
        quarter = self.rows // 4
        start = half * 2 * quarter + (quarter if part == 2 else 0)
        size = 2 * quarter if part == 0 else quarter
        ref = self.buf.at[self.plane.at(half, da, db), pl.ds(start, size), :]
        return pltpu.make_async_remote_copy(
            src_ref=ref,
            dst_ref=ref,
            send_sem=self.ssem,
            recv_sem=self.rsem.at[half * 20 + event],
            device_id={"mp": self.plane.peer(half, ring, step)},
            device_id_type=MESH,
        )

    def own(self, half):
        self.copy(half, 0, 0, 1, 0, 0, 0).start()
        self.copy(half, 1, 0, -1, 0, 0, 0).start()
        self.across(half, 0)

    def across(self, half, k):
        self.copy(half, 4 + 4 * k, 1, 1, OFFS[k], 0, 0).start()
        self.copy(half, 5 + 4 * k, 1, -1, OFFS[k], 0, 0).start()

    def first(self, half):
        self.copy(half, 0, 0, 1, -1, 0, 0).wait_recv()
        self.copy(half, 2, 0, 1, -1, 0, 1).start()
        self.across(half, 1)
        self.copy(half, 1, 0, -1, 1, 0, 0).wait_recv()
        self.copy(half, 3, 0, -1, 1, 0, 2).start()
        self.across(half, 2)

    def second(self, half):
        self.copy(half, 2, 0, 1, 2, 0, 1).wait_recv()
        self.copy(half, 3, 0, -1, 2, 0, 2).wait_recv()
        self.across(half, 3)

    def pass_on(self, half, k):
        self.copy(half, 4 + 4 * k, 1, 1, OFFS[k], -1, 0).wait_recv()
        self.copy(half, 6 + 4 * k, 1, 1, OFFS[k], -1, 1).start()
        self.copy(half, 5 + 4 * k, 1, -1, OFFS[k], 1, 0).wait_recv()
        self.copy(half, 7 + 4 * k, 1, -1, OFFS[k], 1, 2).start()

    def last(self, half, k):
        self.copy(half, 6 + 4 * k, 1, 1, OFFS[k], 2, 1).wait_recv()
        self.copy(half, 7 + 4 * k, 1, -1, OFFS[k], 2, 2).wait_recv()

    def sent(self):
        ref = self.buf.at[pl.ds(0, SIDE * SIDE - 1)]
        pltpu.make_async_copy(ref, ref, self.ssem).wait()


class RingSum:
    def __init__(self, plane, half, ring, src, relay, acc, dst, ssem, rsem):
        self.plane, self.half, self.ring = plane, half, ring
        self.src, self.relay, self.acc, self.dst = src, relay, acc, dst
        self.ssem, self.rsem = ssem, rsem
        self.cut = src.shape[1] // 2

    def copy(self, event):
        step = (1, -1)[event % 2]
        src, dst = self.src, self.dst
        lo, hi = pl.ds(0, self.cut), pl.ds(self.cut, self.cut)
        source, target = (
            lambda: (src.at[3, lo], self.relay.at[0]),
            lambda: (src.at[3, hi], self.relay.at[1]),
            lambda: (src.at[2, hi], dst.at[0, hi]),
            lambda: (src.at[1, lo], dst.at[1, lo]),
            lambda: (self.acc.at[0], dst.at[0, lo]),
            lambda: (self.acc.at[1], dst.at[1, hi]),
        )[event]()
        return pltpu.make_async_remote_copy(
            src_ref=source,
            dst_ref=target,
            send_sem=self.ssem,
            recv_sem=self.rsem.at[event],
            device_id={"mp": self.plane.peer(self.half, self.ring, step)},
            device_id_type=MESH,
        )

    def far(self):
        self.copy(0).start()
        self.copy(1).start()

    def near(self):
        self.copy(2).start()
        self.copy(3).start()

    def join(self):
        lo, hi = pl.ds(0, self.cut), pl.ds(self.cut, self.cut)
        self.copy(0).wait_recv()
        self.acc[0] = (self.src[2, lo].astype(F32) + self.relay[0].astype(F32)).astype(BF16)
        self.copy(4).start()
        self.copy(1).wait_recv()
        self.acc[1] = (self.src[1, hi].astype(F32) + self.relay[1].astype(F32)).astype(BF16)
        self.copy(5).start()

    def arrive(self):
        for event in range(2, 6):
            self.copy(event).wait_recv()

    def sent(self):
        ref = self.src.at[pl.ds(0, 3)]
        pltpu.make_async_copy(ref, ref, self.ssem).wait()


def body(
    matches_ref, actions_ref, state_ref, embed_ref, w_in_hbm, w_out_hbm, head_hbm,
    out_ref,
    zsend0, zsend1, asend, aland, xbuf0, xbuf1, hown, hbuf, w_in, w_out, hid,
    part, relay, acc, dst, sub, srelay, sacc, sdst, keep,
    raw, lsub, lrelay, lacc, ldst, ssend, sland,
    rsend, rland,
    wsem, zsend_sem, zland_sem, asem, hsem, hssem, grsem, gssem, rs_s, rs_r, sq_s, sq_r, bsem,
):
    plane = Plane()
    mp = plane.mp
    sections = lax.axis_size("section")
    me = lax.axis_index("section")
    games = matches_ref.shape[1]
    rows = 2 * games
    cap = zsend0.shape[1]
    agents = sections
    chunks = SIDE * SIDE
    per = sections // chunks
    zsends, xbufs = (zsend0, zsend1), (xbuf0, xbuf1)
    turn = plane.x * SIDE + plane.y
    width = embed_ref.shape[1]
    features = width * chunks

    def other(i):
        k = sections - i
        odd, far = lax.rem(k, 2), (k + 1) // 2
        return lax.rem(me + odd * far + (1 - odd) * (sections - far), sections)

    barrier = pltpu.get_barrier_semaphore()

    def greet(i, _):
        pl.semaphore_signal(barrier, inc=1, device_id={"section": other(i)}, device_id_type=MESH)
        return 0

    lax.fori_loop(1, sections, greet, 0)
    for ring in (0, 1):
        for step in (1, -1):
            pl.semaphore_signal(
                barrier, inc=1, device_id={"mp": plane.peer(0, ring, step)}, device_id_type=MESH
            )
    pl.semaphore_signal(barrier, inc=1, device_id={"mp": plane.peer(0, 1, 2)}, device_id_type=MESH)

    quarter = features // SIDE
    loads = [
        pltpu.make_async_copy(head_hbm.at[:, pl.ds(f * quarter, quarter)], hown.at[f], wsem.at[f])
        for f in range(SIDE)
    ]
    loads.append(pltpu.make_async_copy(w_in_hbm, w_in, wsem.at[SIDE]))
    loads.append(pltpu.make_async_copy(w_out_hbm, w_out, wsem.at[SIDE + 1]))
    for load in loads:
        load.start()

    sub_id = lax.broadcasted_iota(jnp.int32, (rows, rows), 0)
    lane_id = lax.broadcasted_iota(jnp.int32, (rows, rows), 1)

    def line(values):
        return jnp.concatenate([values[0:1], values[1:2]], axis=1)

    def column(row):
        return jnp.sum(
            jnp.where(sub_id == lane_id, row.astype(F32), 0.0), axis=1, keepdims=True
        ).astype(jnp.int32)

    orow = line(matches_ref[...])
    ocol = column(orow)
    same = orow == ocol
    rank_col = jnp.sum(jnp.where(same & (lane_id < sub_id), 1.0, 0.0), axis=1, keepdims=True).astype(
        jnp.int32
    )
    rank_row = jnp.sum(jnp.where(same & (sub_id < lane_id), 1.0, 0.0), axis=0, keepdims=True).astype(
        jnp.int32
    )
    place = orow * cap + rank_row
    pick = jnp.where(
        lax.broadcasted_iota(jnp.int32, (agents * cap, rows), 0) == place, 1.0, 0.0
    ).astype(BF16)

    def send_off(step, seen):
        routed = jnp.dot(pick, seen.astype(BF16), preferred_element_type=F32).astype(BF16)
        zsends[step][...] = routed.reshape(agents, cap, width)

    view = jnp.concatenate([state_ref[:, 0, :], state_ref[:, 1, :]], axis=0)
    send_off(0, view)

    pl.semaphore_wait(barrier, sections - 1 + 5)

    def landing(step):
        return xbufs[step].at[mp, pl.ds(pl.multiple_of(me * cap, cap), cap), :]

    def route(step):
        def one(i, _):
            agent = other(i)
            pltpu.make_async_remote_copy(
                src_ref=zsends[step].at[agent],
                dst_ref=landing(step),
                send_sem=zsend_sem.at[step],
                recv_sem=zland_sem.at[step],
                device_id={"section": agent},
                device_id_type=MESH,
            ).start()
            return 0

        lax.fori_loop(1, sections, one, 0)
        pltpu.make_async_copy(zsends[step].at[me], landing(step), zland_sem.at[step]).start()

    def routed(step):
        whole = xbufs[step].at[mp]
        pltpu.make_async_copy(whole, whole, zland_sem.at[step]).wait()

    route(0)
    inputs = [Gather(plane, xbufs[t], grsem.at[t], gssem.at[t]) for t in range(2)]
    for f in range(SIDE):
        loads[f].wait()

    def deal(d):
        return pltpu.make_async_remote_copy(
            src_ref=hown.at[wrap(plane.y, d)],
            dst_ref=hbuf.at[plane.y, plane.x],
            send_sem=hssem.at[0],
            recv_sem=hsem.at[d],
            device_id={"mp": wrap(plane.y, d) * SIDE + plane.x},
            device_id_type=MESH,
        )

    def share(event, step, off, start, size):
        ref = hbuf.at[pl.ds(start, size), wrap(plane.x, off)]
        return pltpu.make_async_remote_copy(
            src_ref=ref,
            dst_ref=ref,
            send_sem=hssem.at[1],
            recv_sem=hsem.at[4 + event],
            device_id={"mp": plane.y * SIDE + wrap(plane.x, step)},
            device_id_type=MESH,
        )

    for d in (1, 2, 3):
        deal(d).start()
    own_head = pltpu.make_async_copy(hown.at[plane.y], hbuf.at[plane.y, plane.x], hsem.at[0])
    own_head.start()

    act_now, act_next = column(line(actions_ref[0])), column(line(actions_ref[1]))
    act_other = jnp.concatenate([act_now[games:], act_now[:games]], axis=0)
    table = lax.broadcasted_iota(jnp.int32, (rows, embed_ref.shape[0]), 1)
    mix = jnp.where(table == act_now, 1.0, 0.0) + jnp.where(
        table == act_other, 0.5, 0.0
    )
    later = 0.8 * view + jnp.dot(mix.astype(BF16), embed_ref[...], preferred_element_type=F32)
    send_off(1, later)
    route(1)

    owner = jnp.where(lax.broadcasted_iota(jnp.int32, (agents, rows), 0) == orow, 1.0, 0.0)
    spot = lax.broadcasted_iota(jnp.int32, (rows, 128), 1)
    value = jnp.where(spot < cap, act_now, act_next)
    hit = (jnp.where(spot < cap, spot, spot - cap) == rank_col) & (spot < STEPS * cap)
    high = jnp.where(hit, value // 32, 0).astype(F32).astype(BF16)
    low = jnp.where(hit, value % 32, 0).astype(F32).astype(BF16)
    owner16 = owner.astype(BF16)
    named = 32.0 * jnp.dot(owner16, high, preferred_element_type=F32) + jnp.dot(
        owner16, low, preferred_element_type=F32
    )
    asend[...] = named.reshape(agents, 1, 128)

    def tell(i, _):
        agent = other(i)
        pltpu.make_async_remote_copy(
            src_ref=asend.at[agent],
            dst_ref=aland.at[lax.rem(me, per)],
            send_sem=asem.at[0],
            recv_sem=asem.at[1],
            device_id={"section": agent},
            device_id_type=MESH,
        ).start()
        return 0

    @pl.when(me // per == turn)
    def _():
        lax.fori_loop(1, sections, tell, 0)
        pltpu.make_async_copy(asend.at[me], aland.at[lax.rem(me, per)], asem.at[1]).start()

    def open_up(gather):
        for half in (0, 1):
            gather.first(half)
        for half in (0, 1):
            gather.pass_on(half, 0)
        for half in (0, 1):
            gather.second(half)

    def go_on(gather, k):
        for half in (0, 1):
            gather.pass_on(half, k)

    def close(gather):
        for half in (0, 1):
            for k in range(4):
                gather.last(half, k)

    own_head.wait()
    for d in (1, 2, 3):
        deal(d).wait_recv()
    share(0, 1, 0, 0, SIDE).start()
    share(1, -1, 0, 0, SIDE).start()
    routed(0)
    for half in (0, 1):
        inputs[0].own(half)
    share(0, 1, -1, 0, SIDE).wait_recv()
    share(2, 1, -1, 0, SIDE // 2).start()
    share(1, -1, 1, 0, SIDE).wait_recv()
    share(3, -1, 1, SIDE // 2, SIDE // 2).start()
    for half in (0, 1):
        inputs[0].first(half)
    for half in (0, 1):
        inputs[0].pass_on(half, 0)
    routed(1)
    for half in (0, 1):
        inputs[1].own(half)
    for half in (0, 1):
        inputs[0].second(half)
    open_up(inputs[1])
    for t in range(2):
        for k in (1, 2, 3):
            go_on(inputs[t], k)
    loads[SIDE].wait()
    loads[SIDE + 1].wait()

    each = agents * cap // chunks
    span = agents * cap // 2

    def project(t, half):
        lhs = jnp.concatenate([xbufs[t][i, half * span:(half + 1) * span, :] for i in range(chunks)], axis=1)
        total = jnp.dot(lhs, w_in[...], preferred_element_type=F32)
        wide = lhs.astype(F32)
        scale = lax.rsqrt(jnp.sum(wide * wide, axis=1, keepdims=True) * (1.0 / features) + EPS)
        hidden = jax.nn.gelu(total * scale).astype(BF16)
        hid[t, half * chunks // 2:(half + 1) * chunks // 2] = hidden.reshape(
            chunks // 2, each, hidden.shape[1]
        )

    outer = [
        [
            RingSum(
                plane, half, 0, part.at[2 * t + half], relay.at[2 * t + half], acc.at[2 * t + half],
                dst.at[2 * t + half], rs_s.at[2 * t + half], rs_r.at[2 * t + half],
            )
            for half in (0, 1)
        ]
        for t in range(2)
    ]
    inner = [
        [
            RingSum(
                plane, half, 1, sub.at[2 * t + half], srelay.at[2 * t + half], sacc.at[2 * t + half],
                sdst.at[2 * t + half], rs_s.at[4 + 2 * t + half], rs_r.at[4 + 2 * t + half],
            )
            for half in (0, 1)
        ]
        for t in range(2)
    ]

    def nearness(place, pos):
        d = lax.rem(place + SIDE - pos, SIDE)
        return (lax.rem(d, 3) + 1) * jnp.minimum(d, 1)

    def expand(t, half):
        pair = [c * SIDE + 2 * half + b for c in range(SIDE) for b in range(2)]
        lhs = jnp.concatenate([hid[t, i] for i in pair], axis=0)
        total = jnp.dot(lhs, w_out[...], preferred_element_type=F32).astype(BF16)
        for c in range(SIDE):
            for f in range(SIDE):
                piece = total[c * 2 * each:(c + 1) * 2 * each, f * quarter:(f + 1) * quarter]
                if half == 0:
                    part[2 * t + half, nearness(c, plane.x), f] = piece
                else:
                    part[2 * t + half, nearness(f, plane.y), c] = piece

    def spread_out(t):
        for half in (0, 1):
            expand(t, half)
            outer[t][half].far()
            outer[t][half].near()

    def fold(t, half, k):
        b = wrap(plane.y if half == 0 else plane.x, OFFS[k])
        i = 2 * t + half
        return part[i, 0, b].astype(F32) + dst[i, 0, b].astype(F32) + dst[i, 1, b].astype(F32)

    def narrow(t):
        for half in (0, 1):
            i = 2 * t + half
            outer[t][half].arrive()
            sub[i, 3] = fold(t, half, 3).astype(BF16)
            inner[t][half].far()
            sub[i, 1] = fold(t, half, 1).astype(BF16)
            sub[i, 2] = fold(t, half, 2).astype(BF16)
            inner[t][half].near()
            keep[i] = fold(t, half, 0)

    def joined(rings):
        for half in (0, 1):
            rings[half].join()

    ident = lax.broadcasted_iota(jnp.int32, (cap, 128), 0) == lax.broadcasted_iota(
        jnp.int32, (cap, 128), 1
    )
    later_ident = lax.broadcasted_iota(jnp.int32, (cap, 128), 0) + cap == lax.broadcasted_iota(
        jnp.int32, (cap, 128), 1
    )

    logit_sums = [
        RingSum(
            plane, 0, 1, lsub.at[t], lrelay.at[t], lacc.at[t], ldst.at[t], rs_s.at[8 + t], rs_r.at[8 + t]
        )
        for t in range(2)
    ]
    strip = SIDE * each
    diagonal = lax.broadcasted_iota(jnp.int32, (strip, strip), 0) == lax.broadcasted_iota(
        jnp.int32, (strip, strip), 1
    )

    def square_copy(t, d):
        return pltpu.make_async_remote_copy(
            src_ref=ssend.at[t],
            dst_ref=sland.at[t, d - 1],
            send_sem=sq_s.at[t],
            recv_sem=sq_r.at[3 * t + d - 1],
            device_id={"mp": wrap(plane.y, d) * SIDE + plane.x},
            device_id_type=MESH,
        )

    def half_score(t):
        rest = []
        for half in (0, 1):
            i = 2 * t + half
            inner[t][half].arrive()
            rest.append(keep[i] + sdst[i, 0].astype(F32) + sdst[i, 1].astype(F32))
        mine = pl.ds(pl.multiple_of(plane.x * strip, strip), strip)
        source = jnp.concatenate(
            [xbufs[t][plane.y * SIDE + j, mine, :] for j in range(SIDE)], axis=1
        ).astype(F32)
        summed = source + jnp.concatenate(rest, axis=0)
        squares = jnp.sum(summed * summed, axis=1, keepdims=True)
        ssend[t] = jnp.sum(jnp.where(diagonal, squares, 0.0), axis=0, keepdims=True)
        for d in (1, 2, 3):
            square_copy(t, d).start()
        scores = lax.dot_general(
            summed.astype(BF16),
            hbuf[...].reshape(chunks * hbuf.shape[2], quarter),
            (((1,), (1,)), ((), ())),
            preferred_element_type=F32,
        )
        raw[t] = scores.reshape(SIDE, each, scores.shape[1])
        for k in (1, 2, 3):
            lsub[t, k] = raw[t, wrap(plane.y, OFFS[k])].astype(BF16)
        logit_sums[t].far()
        logit_sums[t].near()

    def score(t):
        logit_sums[t].arrive()
        for d in (1, 2, 3):
            square_copy(t, d).wait_recv()
        row = ssend[t] + sland[t, 0] + sland[t, 1] + sland[t, 2]
        at_row = lax.broadcasted_iota(jnp.int32, (each, strip), 1) == (
            lax.broadcasted_iota(jnp.int32, (each, strip), 0) + plane.y * each
        )
        squares = jnp.sum(jnp.where(at_row, row, 0.0), axis=1, keepdims=True)
        scale = lax.rsqrt(squares * (1.0 / features) + EPS)
        scores = scale * (raw[t, plane.y] + ldst[t, 0].astype(F32) + ldst[t, 1].astype(F32))
        peak = jnp.max(scores, axis=1, keepdims=True)
        total = jnp.sum(jnp.exp(scores - peak), axis=1, keepdims=True)
        eye = later_ident if t else ident
        chosen = jnp.concatenate(
            [jnp.sum(jnp.where(eye, aland[c], 0.0), axis=1, keepdims=True) for c in range(per)], axis=0
        )
        names = lax.broadcasted_iota(jnp.int32, scores.shape, 1)
        taken = jnp.sum(
            jnp.where(names == chosen.astype(jnp.int32), scores, 0.0), axis=1, keepdims=True
        )
        logp = taken - peak - jnp.log(total)
        return [
            jnp.sum(jnp.where(eye, logp[c * cap:(c + 1) * cap], 0.0), axis=0, keepdims=True)
            for c in range(per)
        ]

    def give(i, _):
        c = i // chunks
        dest = lax.rem(i, chunks)
        stays = (turn * per + c == me) & (dest == mp)

        @pl.when(jnp.logical_not(stays))
        def _():
            pltpu.make_async_remote_copy(
                src_ref=rsend.at[c],
                dst_ref=rland.at[me],
                send_sem=bsem.at[0],
                recv_sem=bsem.at[1],
                device_id={"section": turn * per + c, "mp": dest},
                device_id_type=MESH,
            ).start()

        @pl.when(stays)
        def _():
            pltpu.make_async_copy(rsend.at[c], rland.at[me], bsem.at[1]).start()

        return 0

    close(inputs[0])
    project(0, 0)
    project(0, 1)
    spread_out(0)
    close(inputs[1])
    project(1, 0)
    project(1, 1)
    spread_out(1)
    joined(outer[0])
    joined(outer[1])
    narrow(0)
    narrow(1)
    joined(inner[0])
    joined(inner[1])
    share(2, 1, 2, 0, SIDE // 2).wait_recv()
    share(3, -1, 2, SIDE // 2, SIDE // 2).wait_recv()
    half_score(0)
    half_score(1)
    joined(logit_sums)
    pltpu.make_async_copy(aland, aland, asem.at[1]).wait()
    found = [score(t) for t in range(2)]
    for c in range(per):
        rsend[c] = found[0][c] + found[1][c]
    lax.fori_loop(0, per * chunks, give, 0)
    pltpu.make_async_copy(rland, rland, bsem.at[1]).wait()
    spread = lax.dot_general(
        rland[...].reshape(agents, 128), owner, (((0,), (0,)), ((), ())),
        precision=lax.Precision.HIGHEST, preferred_element_type=F32,
    )
    slot = lax.broadcasted_iota(jnp.int32, (128, rows), 0)
    for t in range(STEPS):
        value = jnp.sum(jnp.where(slot == rank_row + t * cap, spread, 0.0), axis=0, keepdims=True)
        for player in range(2):
            out_ref[t, player:player + 1, :] = value[:, player * games:(player + 1) * games]

    for step in range(STEPS):
        full = zsends[step].at[pl.ds(0, sections - 1)]
        pltpu.make_async_copy(full, full, zsend_sem.at[step]).wait()

    @pl.when(me // per == turn)
    def _():
        told = asend.at[pl.ds(0, sections - 1)]
        pltpu.make_async_copy(told, told, asem.at[0]).wait()

    dealt = hown.at[pl.ds(0, 3)]
    pltpu.make_async_copy(dealt, dealt, hssem.at[0]).wait()
    shared = hbuf.at[pl.ds(0, 3)]
    pltpu.make_async_copy(shared, shared, hssem.at[1]).wait()
    for t in range(2):
        inputs[t].sent()
        for half in (0, 1):
            outer[t][half].sent()
            inner[t][half].sent()
        logit_sums[t].sent()
        told = sland.at[t]
        pltpu.make_async_copy(told, told, sq_s.at[t]).wait()
    given = rland.at[pl.ds(0, per * chunks - 1)]
    pltpu.make_async_copy(given, given, bsem.at[0]).wait()

    @pl.when(me // per != turn)
    def _():
        one = rland.at[0]
        pltpu.make_async_copy(one, one, bsem.at[0]).wait()


def per_device(matches, actions, state, embed, w_in, w_out, head):
    sections = lax.axis_size("section")
    games = matches.shape[0]
    width = state.shape[2]
    cap = 4 * games // sections
    served = sections * cap
    chunks = SIDE * SIDE
    each = served // chunks
    hidden = w_in.shape[3]
    features = w_in.shape[2]
    columns = head.shape[2]
    quarter = features // SIDE
    actions_all = columns * chunks
    vmem = pl.BlockSpec(memory_space=pltpu.VMEM)
    hbm = pl.BlockSpec(memory_space=pl.ANY)
    per = sections // chunks
    dma = pltpu.SemaphoreType.DMA
    out = pl.pallas_call(
        body,
        out_shape=jax.ShapeDtypeStruct((STEPS, 2, games), F32),
        in_specs=[vmem] * 4 + [hbm] * 3,
        out_specs=vmem,
        scratch_shapes=[
            pltpu.VMEM((sections, cap, width), BF16),
            pltpu.VMEM((sections, cap, width), BF16),
            pltpu.VMEM((sections, 1, 128), F32),
            pltpu.VMEM((per, 1, 128), F32),
            pltpu.VMEM((chunks, served, width), BF16),
            pltpu.VMEM((chunks, served, width), BF16),
            pltpu.VMEM((SIDE, columns, quarter), BF16),
            pltpu.VMEM((SIDE, SIDE, columns, quarter), BF16),
            pltpu.VMEM((features, hidden), BF16),
            pltpu.VMEM((hidden, features), BF16),
            pltpu.VMEM((2, chunks, each, hidden), BF16),
            pltpu.VMEM((4, 4, SIDE, 2 * each, quarter), BF16),
            pltpu.VMEM((4, 2, SIDE // 2, 2 * each, quarter), BF16),
            pltpu.VMEM((4, 2, SIDE // 2, 2 * each, quarter), BF16),
            pltpu.VMEM((4, 2, SIDE, 2 * each, quarter), BF16),
            pltpu.VMEM((4, 4, 2 * each, quarter), BF16),
            pltpu.VMEM((4, 2, each, quarter), BF16),
            pltpu.VMEM((4, 2, each, quarter), BF16),
            pltpu.VMEM((4, 2, 2 * each, quarter), BF16),
            pltpu.VMEM((4, 2 * each, quarter), F32),
            pltpu.VMEM((2, SIDE, each, actions_all), F32),
            pltpu.VMEM((2, 4, each, actions_all), BF16),
            pltpu.VMEM((2, 2, each // 2, actions_all), BF16),
            pltpu.VMEM((2, 2, each // 2, actions_all), BF16),
            pltpu.VMEM((2, 2, each, actions_all), BF16),
            pltpu.VMEM((2, 1, SIDE * each), F32),
            pltpu.VMEM((2, 3, 1, SIDE * each), F32),
            pltpu.VMEM((per, 1, 128), F32),
            pltpu.VMEM((sections, 1, 128), F32),
            dma((6,)), dma((2,)), dma((2,)), dma((2,)), dma((8,)), dma((2,)),
            dma((2, 40)), dma((2,)), dma((10,)), dma((10, 6)), dma((2,)), dma((6,)), dma((2,)),
        ],
        compiler_params=pltpu.CompilerParams(
            collective_id=0, has_side_effects=True, vmem_limit_bytes=60 * 1024 * 1024
        ),
        name="league",
    )(matches.T, actions.swapaxes(1, 2), state, embed, w_in[0, 0], w_out[0, 0], head[0].T)
    return out.swapaxes(1, 2)


def solution(mesh):
    return jax.shard_map(
        per_device,
        mesh=mesh,
        in_specs=(
            P("section", None),
            P(None, "section", None),
            P("section", None, "mp"),
            P(None, "mp"),
            P("section", None, None, "mp"),
            P("section", None, "mp", None),
            P("section", None, "mp"),
        ),
        out_specs=P(None, "section", None),
        check_vma=False,
    )
```

```python
import jax
import jax.numpy as jnp
from jax import lax
from jax.experimental import pallas as pl
from jax.experimental.pallas import tpu as pltpu
from jax.sharding import PartitionSpec as P

STEPS = 2
SIDE = 4
EPS = 1e-06
MESH = pl.DeviceIdType.MESH
F32 = jnp.float32
BF16 = jnp.bfloat16

OFFS = (0, -1, 1, 2)


def wrap(pos, off):
    return lax.rem(pos + (off + SIDE), SIDE) if off else pos


class Plane:
    def __init__(self):
        self.mp = lax.axis_index("mp")
        self.y = self.mp // SIDE
        self.x = lax.rem(self.mp, SIDE)

    def at(self, half, da, db):
        if half == 0:
            return wrap(self.y, db) * SIDE + wrap(self.x, da)
        return wrap(self.y, da) * SIDE + wrap(self.x, db)

    def peer(self, half, ring, step):
        return self.at(half, step, 0) if ring == 0 else self.at(half, 0, step)


class Gather:
    def __init__(self, plane, buf, rsem, ssem):
        self.plane, self.buf, self.rsem, self.ssem = plane, buf, rsem, ssem
        self.rows = buf.shape[1]

    def copy(self, half, event, ring, step, da, db, part):
        quarter = self.rows // 4
        start = half * 2 * quarter + (quarter if part == 2 else 0)
        size = 2 * quarter if part == 0 else quarter
        ref = self.buf.at[self.plane.at(half, da, db), pl.ds(start, size), :]
        return pltpu.make_async_remote_copy(
            src_ref=ref,
            dst_ref=ref,
            send_sem=self.ssem,
            recv_sem=self.rsem.at[half * 20 + event],
            device_id={"mp": self.plane.peer(half, ring, step)},
            device_id_type=MESH,
        )

    def own(self, half):
        self.copy(half, 0, 0, 1, 0, 0, 0).start()
        self.copy(half, 1, 0, -1, 0, 0, 0).start()
        self.across(half, 0)

    def across(self, half, k):
        self.copy(half, 4 + 4 * k, 1, 1, OFFS[k], 0, 0).start()
        self.copy(half, 5 + 4 * k, 1, -1, OFFS[k], 0, 0).start()

    def first(self, half):
        self.copy(half, 0, 0, 1, -1, 0, 0).wait_recv()
        self.copy(half, 2, 0, 1, -1, 0, 1).start()
        self.across(half, 1)
        self.copy(half, 1, 0, -1, 1, 0, 0).wait_recv()
        self.copy(half, 3, 0, -1, 1, 0, 2).start()
        self.across(half, 2)

    def second(self, half):
        self.copy(half, 2, 0, 1, 2, 0, 1).wait_recv()
        self.copy(half, 3, 0, -1, 2, 0, 2).wait_recv()
        self.across(half, 3)

    def pass_on(self, half, k):
        self.copy(half, 4 + 4 * k, 1, 1, OFFS[k], -1, 0).wait_recv()
        self.copy(half, 6 + 4 * k, 1, 1, OFFS[k], -1, 1).start()
        self.copy(half, 5 + 4 * k, 1, -1, OFFS[k], 1, 0).wait_recv()
        self.copy(half, 7 + 4 * k, 1, -1, OFFS[k], 1, 2).start()

    def last(self, half, k):
        self.copy(half, 6 + 4 * k, 1, 1, OFFS[k], 2, 1).wait_recv()
        self.copy(half, 7 + 4 * k, 1, -1, OFFS[k], 2, 2).wait_recv()

    def sent(self):
        ref = self.buf.at[pl.ds(0, SIDE * SIDE - 1)]
        pltpu.make_async_copy(ref, ref, self.ssem).wait()


class RingSum:
    def __init__(self, plane, half, ring, src, relay, acc, dst, ssem, rsem):
        self.plane, self.half, self.ring = plane, half, ring
        self.src, self.relay, self.acc, self.dst = src, relay, acc, dst
        self.ssem, self.rsem = ssem, rsem
        self.cut = src.shape[1] // 2

    def copy(self, event):
        step = (1, -1)[event % 2]
        src, dst = self.src, self.dst
        lo, hi = pl.ds(0, self.cut), pl.ds(self.cut, self.cut)
        source, target = (
            lambda: (src.at[3, lo], self.relay.at[0]),
            lambda: (src.at[3, hi], self.relay.at[1]),
            lambda: (src.at[2, hi], dst.at[0, hi]),
            lambda: (src.at[1, lo], dst.at[1, lo]),
            lambda: (self.acc.at[0], dst.at[0, lo]),
            lambda: (self.acc.at[1], dst.at[1, hi]),
        )[event]()
        return pltpu.make_async_remote_copy(
            src_ref=source,
            dst_ref=target,
            send_sem=self.ssem,
            recv_sem=self.rsem.at[event],
            device_id={"mp": self.plane.peer(self.half, self.ring, step)},
            device_id_type=MESH,
        )

    def far(self):
        self.copy(0).start()
        self.copy(1).start()

    def near(self):
        self.copy(2).start()
        self.copy(3).start()

    def join(self):
        lo, hi = pl.ds(0, self.cut), pl.ds(self.cut, self.cut)
        self.copy(0).wait_recv()
        self.acc[0] = (self.src[2, lo].astype(F32) + self.relay[0].astype(F32)).astype(BF16)
        self.copy(4).start()
        self.copy(1).wait_recv()
        self.acc[1] = (self.src[1, hi].astype(F32) + self.relay[1].astype(F32)).astype(BF16)
        self.copy(5).start()

    def arrive(self):
        for event in range(2, 6):
            self.copy(event).wait_recv()

    def sent(self):
        ref = self.src.at[pl.ds(0, 3)]
        pltpu.make_async_copy(ref, ref, self.ssem).wait()


def body(
    matches_ref, actions_ref, state_ref, embed_ref, w_in_hbm, w_out_hbm, head_hbm,
    out_ref,
    zsend0, zsend1, asend, aland, xbuf0, xbuf1, hown, hbuf, w_in, w_out, hid,
    part, relay, acc, dst, sub, srelay, sacc, sdst, keep,
    raw, lsub, lrelay, lacc, ldst, ssend, sland,
    rsend, rland,
    wsem, zsend_sem, zland_sem, asem, hsem, hssem, grsem, gssem, rs_s, rs_r, sq_s, sq_r, bsem,
):
    plane = Plane()
    mp = plane.mp
    sections = lax.axis_size("section")
    me = lax.axis_index("section")
    games = matches_ref.shape[1]
    rows = 2 * games
    cap = zsend0.shape[1]
    agents = sections
    chunks = SIDE * SIDE
    per = sections // chunks
    zsends, xbufs = (zsend0, zsend1), (xbuf0, xbuf1)
    turn = plane.x * SIDE + plane.y
    width = embed_ref.shape[1]
    features = width * chunks

    def other(i):
        k = sections - i
        odd, far = lax.rem(k, 2), (k + 1) // 2
        return lax.rem(me + odd * far + (1 - odd) * (sections - far), sections)

    barrier = pltpu.get_barrier_semaphore()

    def greet(i, _):
        pl.semaphore_signal(barrier, inc=1, device_id={"section": other(i)}, device_id_type=MESH)
        return 0

    lax.fori_loop(1, sections, greet, 0)
    for ring in (0, 1):
        for step in (1, -1):
            pl.semaphore_signal(
                barrier, inc=1, device_id={"mp": plane.peer(0, ring, step)}, device_id_type=MESH
            )
    pl.semaphore_signal(barrier, inc=1, device_id={"mp": plane.peer(0, 1, 2)}, device_id_type=MESH)

    quarter = features // SIDE
    loads = [
        pltpu.make_async_copy(head_hbm.at[:, pl.ds(f * quarter, quarter)], hown.at[f], wsem.at[f])
        for f in range(SIDE)
    ]
    loads.append(pltpu.make_async_copy(w_in_hbm, w_in, wsem.at[SIDE]))
    loads.append(pltpu.make_async_copy(w_out_hbm, w_out, wsem.at[SIDE + 1]))
    for load in loads:
        load.start()

    sub_id = lax.broadcasted_iota(jnp.int32, (rows, rows), 0)
    lane_id = lax.broadcasted_iota(jnp.int32, (rows, rows), 1)

    def line(values):
        return jnp.concatenate([values[0:1], values[1:2]], axis=1)

    def column(row):
        return jnp.sum(
            jnp.where(sub_id == lane_id, row.astype(F32), 0.0), axis=1, keepdims=True
        ).astype(jnp.int32)

    orow = line(matches_ref[...])
    ocol = column(orow)
    same = orow == ocol
    rank_col = jnp.sum(jnp.where(same & (lane_id < sub_id), 1.0, 0.0), axis=1, keepdims=True).astype(
        jnp.int32
    )
    rank_row = jnp.sum(jnp.where(same & (sub_id < lane_id), 1.0, 0.0), axis=0, keepdims=True).astype(
        jnp.int32
    )
    place = orow * cap + rank_row
    pick = jnp.where(
        lax.broadcasted_iota(jnp.int32, (agents * cap, rows), 0) == place, 1.0, 0.0
    ).astype(BF16)

    def send_off(step, seen):
        routed = jnp.dot(pick, seen.astype(BF16), preferred_element_type=F32).astype(BF16)
        zsends[step][...] = routed.reshape(agents, cap, width)

    view = jnp.concatenate([state_ref[:, 0, :], state_ref[:, 1, :]], axis=0)
    send_off(0, view)

    pl.semaphore_wait(barrier, sections - 1 + 5)

    def landing(step):
        return xbufs[step].at[mp, pl.ds(pl.multiple_of(me * cap, cap), cap), :]

    def route(step):
        def one(i, _):
            agent = other(i)
            pltpu.make_async_remote_copy(
                src_ref=zsends[step].at[agent],
                dst_ref=landing(step),
                send_sem=zsend_sem.at[step],
                recv_sem=zland_sem.at[step],
                device_id={"section": agent},
                device_id_type=MESH,
            ).start()
            return 0

        lax.fori_loop(1, sections, one, 0)
        pltpu.make_async_copy(zsends[step].at[me], landing(step), zland_sem.at[step]).start()

    def routed(step):
        whole = xbufs[step].at[mp]
        pltpu.make_async_copy(whole, whole, zland_sem.at[step]).wait()

    route(0)
    inputs = [Gather(plane, xbufs[t], grsem.at[t], gssem.at[t]) for t in range(2)]
    for f in range(SIDE):
        loads[f].wait()

    def deal(d):
        return pltpu.make_async_remote_copy(
            src_ref=hown.at[wrap(plane.y, d)],
            dst_ref=hbuf.at[plane.y, plane.x],
            send_sem=hssem.at[0],
            recv_sem=hsem.at[d],
            device_id={"mp": wrap(plane.y, d) * SIDE + plane.x},
            device_id_type=MESH,
        )

    def share(event, step, off, start, size):
        ref = hbuf.at[pl.ds(start, size), wrap(plane.x, off)]
        return pltpu.make_async_remote_copy(
            src_ref=ref,
            dst_ref=ref,
            send_sem=hssem.at[1],
            recv_sem=hsem.at[4 + event],
            device_id={"mp": plane.y * SIDE + wrap(plane.x, step)},
            device_id_type=MESH,
        )

    for d in (1, 2, 3):
        deal(d).start()
    own_head = pltpu.make_async_copy(hown.at[plane.y], hbuf.at[plane.y, plane.x], hsem.at[0])
    own_head.start()

    act_now, act_next = column(line(actions_ref[0])), column(line(actions_ref[1]))
    act_other = jnp.concatenate([act_now[games:], act_now[:games]], axis=0)
    table = lax.broadcasted_iota(jnp.int32, (rows, embed_ref.shape[0]), 1)
    mix = jnp.where(table == act_now, 1.0, 0.0) + jnp.where(
        table == act_other, 0.5, 0.0
    )
    later = 0.8 * view + jnp.dot(mix.astype(BF16), embed_ref[...], preferred_element_type=F32)
    send_off(1, later)
    route(1)

    owner = jnp.where(lax.broadcasted_iota(jnp.int32, (agents, rows), 0) == orow, 1.0, 0.0)
    spot = lax.broadcasted_iota(jnp.int32, (rows, 128), 1)
    value = jnp.where(spot < cap, act_now, act_next)
    hit = (jnp.where(spot < cap, spot, spot - cap) == rank_col) & (spot < STEPS * cap)
    high = jnp.where(hit, value // 32, 0).astype(F32).astype(BF16)
    low = jnp.where(hit, value % 32, 0).astype(F32).astype(BF16)
    owner16 = owner.astype(BF16)
    named = 32.0 * jnp.dot(owner16, high, preferred_element_type=F32) + jnp.dot(
        owner16, low, preferred_element_type=F32
    )
    asend[...] = named.reshape(agents, 1, 128)

    def tell(i, _):
        agent = other(i)
        pltpu.make_async_remote_copy(
            src_ref=asend.at[agent],
            dst_ref=aland.at[lax.rem(me, per)],
            send_sem=asem.at[0],
            recv_sem=asem.at[1],
            device_id={"section": agent},
            device_id_type=MESH,
        ).start()
        return 0

    @pl.when(me // per == turn)
    def _():
        lax.fori_loop(1, sections, tell, 0)
        pltpu.make_async_copy(asend.at[me], aland.at[lax.rem(me, per)], asem.at[1]).start()

    def open_up(gather):
        for half in (0, 1):
            gather.first(half)
        for half in (0, 1):
            gather.pass_on(half, 0)
        for half in (0, 1):
            gather.second(half)

    def go_on(gather, k):
        for half in (0, 1):
            gather.pass_on(half, k)

    def close(gather):
        for half in (0, 1):
            for k in range(4):
                gather.last(half, k)

    own_head.wait()
    for d in (1, 2, 3):
        deal(d).wait_recv()
    share(0, 1, 0, 0, SIDE).start()
    share(1, -1, 0, 0, SIDE).start()
    routed(0)
    for half in (0, 1):
        inputs[0].own(half)
    for half in (0, 1):
        inputs[0].first(half)
    for half in (0, 1):
        inputs[0].pass_on(half, 0)
    routed(1)
    for half in (0, 1):
        inputs[1].own(half)
    for half in (0, 1):
        inputs[0].second(half)
    open_up(inputs[1])
    for t in range(2):
        for k in (1, 2, 3):
            go_on(inputs[t], k)
    share(0, 1, -1, 0, SIDE).wait_recv()
    share(2, 1, -1, 0, SIDE // 2).start()
    share(1, -1, 1, 0, SIDE).wait_recv()
    share(3, -1, 1, SIDE // 2, SIDE // 2).start()
    loads[SIDE].wait()
    loads[SIDE + 1].wait()

    each = agents * cap // chunks
    span = agents * cap // 2

    def project(t, half):
        lhs = jnp.concatenate([xbufs[t][i, half * span:(half + 1) * span, :] for i in range(chunks)], axis=1)
        total = jnp.dot(lhs, w_in[...], preferred_element_type=F32)
        wide = lhs.astype(F32)
        scale = lax.rsqrt(jnp.sum(wide * wide, axis=1, keepdims=True) * (1.0 / features) + EPS)
        hidden = jax.nn.gelu(total * scale).astype(BF16)
        hid[t, half * chunks // 2:(half + 1) * chunks // 2] = hidden.reshape(
            chunks // 2, each, hidden.shape[1]
        )

    outer = [
        [
            RingSum(
                plane, half, 0, part.at[2 * t + half], relay.at[2 * t + half], acc.at[2 * t + half],
                dst.at[2 * t + half], rs_s.at[2 * t + half], rs_r.at[2 * t + half],
            )
            for half in (0, 1)
        ]
        for t in range(2)
    ]
    inner = [
        [
            RingSum(
                plane, half, 1, sub.at[2 * t + half], srelay.at[2 * t + half], sacc.at[2 * t + half],
                sdst.at[2 * t + half], rs_s.at[4 + 2 * t + half], rs_r.at[4 + 2 * t + half],
            )
            for half in (0, 1)
        ]
        for t in range(2)
    ]

    def nearness(place, pos):
        d = lax.rem(place + SIDE - pos, SIDE)
        return (lax.rem(d, 3) + 1) * jnp.minimum(d, 1)

    def expand(t, half):
        pair = [c * SIDE + 2 * half + b for c in range(SIDE) for b in range(2)]
        lhs = jnp.concatenate([hid[t, i] for i in pair], axis=0)
        total = jnp.dot(lhs, w_out[...], preferred_element_type=F32).astype(BF16)
        for c in range(SIDE):
            for f in range(SIDE):
                piece = total[c * 2 * each:(c + 1) * 2 * each, f * quarter:(f + 1) * quarter]
                if half == 0:
                    part[2 * t + half, nearness(c, plane.x), f] = piece
                else:
                    part[2 * t + half, nearness(f, plane.y), c] = piece

    def spread_out(t):
        for half in (0, 1):
            expand(t, half)
            outer[t][half].far()
            outer[t][half].near()

    def fold(t, half, k):
        b = wrap(plane.y if half == 0 else plane.x, OFFS[k])
        i = 2 * t + half
        return part[i, 0, b].astype(F32) + dst[i, 0, b].astype(F32) + dst[i, 1, b].astype(F32)

    def narrow(t):
        for half in (0, 1):
            i = 2 * t + half
            outer[t][half].arrive()
            sub[i, 3] = fold(t, half, 3).astype(BF16)
            inner[t][half].far()
            sub[i, 1] = fold(t, half, 1).astype(BF16)
            sub[i, 2] = fold(t, half, 2).astype(BF16)
            inner[t][half].near()
            keep[i] = fold(t, half, 0)

    def joined(rings):
        for half in (0, 1):
            rings[half].join()

    ident = lax.broadcasted_iota(jnp.int32, (cap, 128), 0) == lax.broadcasted_iota(
        jnp.int32, (cap, 128), 1
    )
    later_ident = lax.broadcasted_iota(jnp.int32, (cap, 128), 0) + cap == lax.broadcasted_iota(
        jnp.int32, (cap, 128), 1
    )

    logit_sums = [
        RingSum(
            plane, 0, 1, lsub.at[t], lrelay.at[t], lacc.at[t], ldst.at[t], rs_s.at[8 + t], rs_r.at[8 + t]
        )
        for t in range(2)
    ]
    strip = SIDE * each
    diagonal = lax.broadcasted_iota(jnp.int32, (strip, strip), 0) == lax.broadcasted_iota(
        jnp.int32, (strip, strip), 1
    )

    def square_copy(t, d):
        return pltpu.make_async_remote_copy(
            src_ref=ssend.at[t],
            dst_ref=sland.at[t, d - 1],
            send_sem=sq_s.at[t],
            recv_sem=sq_r.at[3 * t + d - 1],
            device_id={"mp": wrap(plane.y, d) * SIDE + plane.x},
            device_id_type=MESH,
        )

    def half_score(t):
        rest = []
        for half in (0, 1):
            i = 2 * t + half
            inner[t][half].arrive()
            rest.append(keep[i] + sdst[i, 0].astype(F32) + sdst[i, 1].astype(F32))
        mine = pl.ds(pl.multiple_of(plane.x * strip, strip), strip)
        source = jnp.concatenate(
            [xbufs[t][plane.y * SIDE + j, mine, :] for j in range(SIDE)], axis=1
        ).astype(F32)
        summed = source + jnp.concatenate(rest, axis=0)
        squares = jnp.sum(summed * summed, axis=1, keepdims=True)
        ssend[t] = jnp.sum(jnp.where(diagonal, squares, 0.0), axis=0, keepdims=True)
        for d in (1, 2, 3):
            square_copy(t, d).start()
        scores = lax.dot_general(
            summed.astype(BF16),
            hbuf[...].reshape(chunks * hbuf.shape[2], quarter),
            (((1,), (1,)), ((), ())),
            preferred_element_type=F32,
        )
        raw[t] = scores.reshape(SIDE, each, scores.shape[1])
        for k in (1, 2, 3):
            lsub[t, k] = raw[t, wrap(plane.y, OFFS[k])].astype(BF16)
        logit_sums[t].far()
        logit_sums[t].near()

    def score(t):
        logit_sums[t].arrive()
        for d in (1, 2, 3):
            square_copy(t, d).wait_recv()
        row = ssend[t] + sland[t, 0] + sland[t, 1] + sland[t, 2]
        at_row = lax.broadcasted_iota(jnp.int32, (each, strip), 1) == (
            lax.broadcasted_iota(jnp.int32, (each, strip), 0) + plane.y * each
        )
        squares = jnp.sum(jnp.where(at_row, row, 0.0), axis=1, keepdims=True)
        scale = lax.rsqrt(squares * (1.0 / features) + EPS)
        scores = scale * (raw[t, plane.y] + ldst[t, 0].astype(F32) + ldst[t, 1].astype(F32))
        peak = jnp.max(scores, axis=1, keepdims=True)
        total = jnp.sum(jnp.exp(scores - peak), axis=1, keepdims=True)
        eye = later_ident if t else ident
        chosen = jnp.concatenate(
            [jnp.sum(jnp.where(eye, aland[c], 0.0), axis=1, keepdims=True) for c in range(per)], axis=0
        )
        names = lax.broadcasted_iota(jnp.int32, scores.shape, 1)
        taken = jnp.sum(
            jnp.where(names == chosen.astype(jnp.int32), scores, 0.0), axis=1, keepdims=True
        )
        logp = taken - peak - jnp.log(total)
        return [
            jnp.sum(jnp.where(eye, logp[c * cap:(c + 1) * cap], 0.0), axis=0, keepdims=True)
            for c in range(per)
        ]

    def give(i, _):
        c = i // chunks
        dest = lax.rem(i, chunks)
        stays = (turn * per + c == me) & (dest == mp)

        @pl.when(jnp.logical_not(stays))
        def _():
            pltpu.make_async_remote_copy(
                src_ref=rsend.at[c],
                dst_ref=rland.at[me],
                send_sem=bsem.at[0],
                recv_sem=bsem.at[1],
                device_id={"section": turn * per + c, "mp": dest},
                device_id_type=MESH,
            ).start()

        @pl.when(stays)
        def _():
            pltpu.make_async_copy(rsend.at[c], rland.at[me], bsem.at[1]).start()

        return 0

    close(inputs[0])
    project(0, 0)
    project(0, 1)
    spread_out(0)
    close(inputs[1])
    project(1, 0)
    project(1, 1)
    spread_out(1)
    joined(outer[0])
    joined(outer[1])
    narrow(0)
    narrow(1)
    joined(inner[0])
    joined(inner[1])
    share(2, 1, 2, 0, SIDE // 2).wait_recv()
    share(3, -1, 2, SIDE // 2, SIDE // 2).wait_recv()
    half_score(0)
    half_score(1)
    joined(logit_sums)
    pltpu.make_async_copy(aland, aland, asem.at[1]).wait()
    found = [score(t) for t in range(2)]
    for c in range(per):
        rsend[c] = found[0][c] + found[1][c]
    lax.fori_loop(0, per * chunks, give, 0)
    pltpu.make_async_copy(rland, rland, bsem.at[1]).wait()
    spread = lax.dot_general(
        rland[...].reshape(agents, 128), owner, (((0,), (0,)), ((), ())),
        precision=lax.Precision.HIGHEST, preferred_element_type=F32,
    )
    slot = lax.broadcasted_iota(jnp.int32, (128, rows), 0)
    for t in range(STEPS):
        value = jnp.sum(jnp.where(slot == rank_row + t * cap, spread, 0.0), axis=0, keepdims=True)
        for player in range(2):
            out_ref[t, player:player + 1, :] = value[:, player * games:(player + 1) * games]

    for step in range(STEPS):
        full = zsends[step].at[pl.ds(0, sections - 1)]
        pltpu.make_async_copy(full, full, zsend_sem.at[step]).wait()

    @pl.when(me // per == turn)
    def _():
        told = asend.at[pl.ds(0, sections - 1)]
        pltpu.make_async_copy(told, told, asem.at[0]).wait()

    dealt = hown.at[pl.ds(0, 3)]
    pltpu.make_async_copy(dealt, dealt, hssem.at[0]).wait()
    shared = hbuf.at[pl.ds(0, 3)]
    pltpu.make_async_copy(shared, shared, hssem.at[1]).wait()
    for t in range(2):
        inputs[t].sent()
        for half in (0, 1):
            outer[t][half].sent()
            inner[t][half].sent()
        logit_sums[t].sent()
        told = sland.at[t]
        pltpu.make_async_copy(told, told, sq_s.at[t]).wait()
    given = rland.at[pl.ds(0, per * chunks - 1)]
    pltpu.make_async_copy(given, given, bsem.at[0]).wait()

    @pl.when(me // per != turn)
    def _():
        one = rland.at[0]
        pltpu.make_async_copy(one, one, bsem.at[0]).wait()


def per_device(matches, actions, state, embed, w_in, w_out, head):
    sections = lax.axis_size("section")
    games = matches.shape[0]
    width = state.shape[2]
    cap = 4 * games // sections
    served = sections * cap
    chunks = SIDE * SIDE
    each = served // chunks
    hidden = w_in.shape[3]
    features = w_in.shape[2]
    columns = head.shape[2]
    quarter = features // SIDE
    actions_all = columns * chunks
    vmem = pl.BlockSpec(memory_space=pltpu.VMEM)
    hbm = pl.BlockSpec(memory_space=pl.ANY)
    per = sections // chunks
    dma = pltpu.SemaphoreType.DMA
    out = pl.pallas_call(
        body,
        out_shape=jax.ShapeDtypeStruct((STEPS, 2, games), F32),
        in_specs=[vmem] * 4 + [hbm] * 3,
        out_specs=vmem,
        scratch_shapes=[
            pltpu.VMEM((sections, cap, width), BF16),
            pltpu.VMEM((sections, cap, width), BF16),
            pltpu.VMEM((sections, 1, 128), F32),
            pltpu.VMEM((per, 1, 128), F32),
            pltpu.VMEM((chunks, served, width), BF16),
            pltpu.VMEM((chunks, served, width), BF16),
            pltpu.VMEM((SIDE, columns, quarter), BF16),
            pltpu.VMEM((SIDE, SIDE, columns, quarter), BF16),
            pltpu.VMEM((features, hidden), BF16),
            pltpu.VMEM((hidden, features), BF16),
            pltpu.VMEM((2, chunks, each, hidden), BF16),
            pltpu.VMEM((4, 4, SIDE, 2 * each, quarter), BF16),
            pltpu.VMEM((4, 2, SIDE // 2, 2 * each, quarter), BF16),
            pltpu.VMEM((4, 2, SIDE // 2, 2 * each, quarter), BF16),
            pltpu.VMEM((4, 2, SIDE, 2 * each, quarter), BF16),
            pltpu.VMEM((4, 4, 2 * each, quarter), BF16),
            pltpu.VMEM((4, 2, each, quarter), BF16),
            pltpu.VMEM((4, 2, each, quarter), BF16),
            pltpu.VMEM((4, 2, 2 * each, quarter), BF16),
            pltpu.VMEM((4, 2 * each, quarter), F32),
            pltpu.VMEM((2, SIDE, each, actions_all), F32),
            pltpu.VMEM((2, 4, each, actions_all), BF16),
            pltpu.VMEM((2, 2, each // 2, actions_all), BF16),
            pltpu.VMEM((2, 2, each // 2, actions_all), BF16),
            pltpu.VMEM((2, 2, each, actions_all), BF16),
            pltpu.VMEM((2, 1, SIDE * each), F32),
            pltpu.VMEM((2, 3, 1, SIDE * each), F32),
            pltpu.VMEM((per, 1, 128), F32),
            pltpu.VMEM((sections, 1, 128), F32),
            dma((6,)), dma((2,)), dma((2,)), dma((2,)), dma((8,)), dma((2,)),
            dma((2, 40)), dma((2,)), dma((10,)), dma((10, 6)), dma((2,)), dma((6,)), dma((2,)),
        ],
        compiler_params=pltpu.CompilerParams(
            collective_id=0, has_side_effects=True, vmem_limit_bytes=60 * 1024 * 1024
        ),
        name="league",
    )(matches.T, actions.swapaxes(1, 2), state, embed, w_in[0, 0], w_out[0, 0], head[0].T)
    return out.swapaxes(1, 2)


def solution(mesh):
    return jax.shard_map(
        per_device,
        mesh=mesh,
        in_specs=(
            P("section", None),
            P(None, "section", None),
            P("section", None, "mp"),
            P(None, "mp"),
            P("section", None, None, "mp"),
            P("section", None, "mp", None),
            P("section", None, "mp"),
        ),
        out_specs=P(None, "section", None),
        check_vma=False,
    )
```
